256 devices in a mesh: seq: 32 (over y, x, z_hi), head: 8 (over z_lo, core).
Axes of the slice: x: 4, y: 4, z: 8 (z_hi: 2, z_lo: 4; z = z_hi * 4 + z_lo), core: 2. Of those that a mesh axis runs over, the one named last changes fastest.
Arguments:
- queries: bfloat16 [16384, 4096], P(('seq', 'head')), may hold values from -72 to 72
- keys: bfloat16 [16384, 2048], P(('seq', 'head')), may hold values from -6 to 6
- values: bfloat16 [16384, 2048], P(('seq', 'head')), may hold values from -6 to 6
- prefix_keys: bfloat16 [4096, 2048], P(None, 'head'), may hold values from -10 to 10
- prefix_values: bfloat16 [4096, 2048], P(None, 'head'), may hold values from -6 to 6
- span_start: int32 [1], replicated, may hold values from 0 to 4095
Outputs:
- attended: bfloat16 [16384, 4096], P(('seq', 'head'))
The draws below stay inside these ranges and needn't reach their ends.
All inputs are finite; a program needn't handle non-finite values.
Results may differ from the reference program's by a relative error of at most 0.003.
Values may be sent and summed in bfloat16 or wider, within the bound.
A program may use at most 128 MiB of HBM per device.

```python
import jax
import jax.numpy as jnp
from jax import lax

HEAD_DIM = 128
QH = 32
KVH = 16
QSCALE = 144
WINDOW = 4096
TOKENS = 16384
BLOCK = 512


def base_keys(key):
    raw = jax.random.normal(jax.random.fold_in(key, 7), (TOKENS, KVH * HEAD_DIM), jnp.float32)
    return jnp.clip(1.7 * raw, -6.0, 6.0)


def draw_keys(key, part):
    result = base_keys(key)
    return result.astype(jnp.bfloat16)


def draw_queries(key, part):
    raw = jax.random.normal(jax.random.fold_in(key, 11), (TOKENS, QH * HEAD_DIM), jnp.float32)
    result = jnp.clip(1.7 * raw, -6.0, 6.0)
    return result.astype(jnp.bfloat16)


def levels(rng, extent, pieces, least, top_value):
    loudness, own = 1.0, jax.random.fold_in(rng, 6)
    for dim, shards_of in pieces:
        steps = jnp.exp(jax.random.uniform(jax.random.fold_in(own, dim), (shards_of,), jnp.float32, least / len(pieces), top_value / len(pieces)))
        loudness = loudness * jnp.repeat(steps, extent[dim] // shards_of).reshape([-1 if axis == dim else 1 for axis in range(len(extent))])
    return loudness


def gaussian(key, shape, deviation, limit, split=(), kind=jnp.bfloat16):
    drawn = jax.random.normal(key, shape, jnp.float32) * deviation
    if len(split) > 0:
        drawn = levels(key, shape, split, -0.22, 0.18) * drawn
    return jnp.clip(drawn, min=-limit, max=limit).astype(kind)


def setup_inputs(seed: int = 0) -> dict:
    arg_keys = jax.random.split(jax.random.key(seed), 7)
    queries = draw_queries(jax.random.fold_in(arg_keys[6], 71), 0)
    keys = draw_keys(jax.random.fold_in(arg_keys[6], 71), 0)
    values = gaussian(arg_keys[2], (TOKENS, KVH * HEAD_DIM), 1.0, 6.0, ((0, 256),))
    prefix_keys = gaussian(arg_keys[3], (WINDOW, KVH * HEAD_DIM), 1.7, 10.0, ((1, 8),))
    prefix_values = gaussian(arg_keys[4], (WINDOW, KVH * HEAD_DIM), 1.0, 6.0, ((1, 8),))
    span_start = jax.random.randint(arg_keys[5], (1,), 0, WINDOW).astype(jnp.int32)
    return {"queries": queries, "keys": keys, "values": values, "prefix_keys": prefix_keys, "prefix_values": prefix_values, "span_start": span_start}


def attend_exact(query_rows, key_rows, value_rows, query_first, key_first, start_value):
    block_rows = query_rows.shape[0]
    key_count = key_rows.shape[0]
    grouping = QH // KVH
    scaling = QSCALE ** -0.5
    query_pos = query_first + jnp.arange(block_rows, dtype=jnp.int32)
    key_pos = key_first + jnp.arange(key_count, dtype=jnp.int32)
    distance = query_pos[:, None] - key_pos[None, :]
    allowed = (distance >= 0) & (distance < WINDOW) & ((start_value + key_pos) >= 0)[None, :]
    outputs = []
    for key_group in range(KVH):
        lower = key_group * grouping * HEAD_DIM
        query_head = query_rows[:, lower:lower + grouping * HEAD_DIM].reshape(block_rows, grouping, HEAD_DIM).astype(jnp.float32)
        key_head = key_rows[:, key_group * HEAD_DIM:(key_group + 1) * HEAD_DIM].astype(jnp.float32)
        value_head = value_rows[:, key_group * HEAD_DIM:(key_group + 1) * HEAD_DIM].astype(jnp.float32)
        scores = jnp.einsum("qgd,kd->gqk", query_head, key_head) * scaling
        scores = jnp.where(allowed[None], scores, -jnp.inf)
        peak_score = jnp.max(scores, axis=2, keepdims=True)
        unnormed = jnp.where(allowed[None], jnp.exp(scores - peak_score), jnp.float32(0.0))
        totals = jnp.sum(unnormed, axis=2)
        weights = lax.optimization_barrier(unnormed.astype(jnp.bfloat16)).astype(jnp.float32)
        mixture = jnp.einsum("gqk,kd->qgd", weights, value_head)
        outputs.append((mixture / jnp.transpose(totals)[:, :, None]).reshape(block_rows, grouping * HEAD_DIM))
    return jnp.concatenate(outputs, axis=1).astype(jnp.bfloat16)


def reference(queries, keys, values, prefix_keys, prefix_values, span_start):
    all_keys = jnp.concatenate([prefix_keys, keys], axis=0)
    all_values = jnp.concatenate([prefix_values, values], axis=0)
    start_value = span_start[0]

    def one_block(block_index):
        first = block_index * BLOCK
        query_rows = lax.dynamic_slice_in_dim(queries, first, BLOCK, 0)
        key_rows = lax.dynamic_slice_in_dim(all_keys, first, WINDOW + BLOCK, 0)
        value_rows = lax.dynamic_slice_in_dim(all_values, first, WINDOW + BLOCK, 0)
        return attend_exact(query_rows, key_rows, value_rows, first, first - WINDOW, start_value)

    blocks = lax.map(one_block, jnp.arange(TOKENS // BLOCK, dtype=jnp.int32))
    return blocks.reshape(TOKENS, QH * HEAD_DIM)
```

```python
import functools
import math

import jax
import jax.numpy as jnp
from jax import lax
from jax.experimental import pallas as pl
from jax.experimental.pallas import tpu as pltpu
from jax.sharding import PartitionSpec as P

HEAD_DIM = 128
QH = 32
KVH = 16
QSCALE = 144
WINDOW = 4096

MESH = pl.DeviceIdType.MESH
ROWS = 64
COLUMN = 1024
PIECE = 256
PIECES = COLUMN // PIECE
SLOTS = 5
SPAN = WINDOW + PIECE
STEPS = SPAN // PIECE
PAIR = 2 * HEAD_DIM
MASKED = -1e30
LOG2E_SCALED = math.log2(math.e) * QSCALE ** (-0.5)
NT = (((1,), (1,)), ((), ()))


def ring_offset(t):
    half = (t + 1) // 2
    return jnp.where(t % 2 == 1, half, -half)


def kernel(
    start_ref, q_ref, k_ref, v_ref, pk_ref, pv_ref, out_ref,
    window, q_in, keys2, values2, q2, scores, peaks, o_out,
    kv_sem, q_sem, o_sem, in_send, fwd_send, prefix_send, o_send,
):
    seq, head = lax.axis_index("seq"), lax.axis_index("head")
    y, x, z = seq // 8, (seq // 2) % 4, (seq % 2) * 4 + head // 2
    core = head % 2
    z_hi = seq % 2
    xp, xl = x // 2, x % 2
    other = 1 - core
    my_column = 2 * xp + core
    flip = (xl + xp) % 2

    def device(y_, x_, z_, core_):
        return (y_ * 8 + x_ * 2 + z_ // 4, (z_ % 4) * 2 + core_)

    def chip_head(x_, z_):
        return (z_ % 4) * 4 + (z_ // 4) * 2 + (x_ % 2 + x_ // 2) % 2

    my_head = chip_head(x, z)
    x_near = 3 - x

    def remote(src, dst, send, recv, to):
        return pltpu.make_async_remote_copy(
            src_ref=src, dst_ref=dst, send_sem=send, recv_sem=recv,
            device_id=to, device_id_type=MESH,
        )

    barrier = pltpu.get_barrier_semaphore()

    def greet(to):
        pl.semaphore_signal(barrier, inc=1, device_id=to, device_id_type=MESH)

    def greet_group(i, carry):
        x_, z_, core_ = 2 * xp + i // 16, (i // 2) % 8, i % 2
        pl.when(jnp.logical_not((x_ == x) & (z_ == z) & (core_ == core)))(
            lambda: greet(device(y, x_, z_, core_))
        )
        return carry

    lax.fori_loop(0, 32, greet_group, 0)
    greet(device(y, x_near, z, core))
    greet(device((y + 1) % 4, x, z, core))
    greet(device((y + 3) % 4, x, z, core))
    pl.semaphore_wait(barrier, 34)

    my_rows = pl.ds(pl.multiple_of((z * 2 + core) * ROWS, ROWS), ROWS)

    def each_target(body):
        def at(t, carry):
            z_ = (z + ring_offset(t) + 8) % 8
            for lane in range(2):
                x_ = 2 * xp + lane
                mine = (t == 0) & (xl == lane) & (core == xl)
                body(t, lane, x_, z_, mine)
            return carry

        lax.fori_loop(0, 8, at, 0)

    def send_kv(t, lane, x_, z_, mine):
        h = chip_head(x_, z_)
        cols = pl.ds(pl.multiple_of(h * HEAD_DIM, HEAD_DIM), HEAD_DIM)
        for n, src in enumerate((k_ref, v_ref)):
            dst = window.at[4, my_rows, pl.ds(n * HEAD_DIM, HEAD_DIM)]
            recv = kv_sem.at[4, z // 2]

            @pl.when(mine)
            def _():
                pltpu.make_async_copy(src.at[:, cols], dst, recv).start()

            @pl.when(jnp.logical_not(mine))
            def _():
                remote(
                    src.at[:, cols], dst, in_send.at[t, lane, n], recv, device(y, x_, z_, xl)
                ).start()

    def send_q(t, lane, x_, z_, mine):
        h = chip_head(x_, z_)
        cols = pl.ds(pl.multiple_of(h * PAIR, PAIR), PAIR)
        dst = q_in.at[my_rows, :]
        recv = q_sem.at[z // 2]

        @pl.when(mine)
        def _():
            pltpu.make_async_copy(q_ref.at[:, cols], dst, recv).start()

        @pl.when(jnp.logical_not(mine))
        def _():
            remote(
                q_ref.at[:, cols], dst, in_send.at[t, lane, 2], recv, device(y, x_, z_, xl)
            ).start()

    def sent(t, lane, x_, z_, mine):
        @pl.when(jnp.logical_not(mine))
        def _():
            to = device(y, x_, z_, xl)
            for n, src in enumerate((k_ref, v_ref)):
                cols = pl.ds(0, HEAD_DIM)
                dst = window.at[4, my_rows, pl.ds(n * HEAD_DIM, HEAD_DIM)]
                remote(src.at[:, cols], dst, in_send.at[t, lane, n], kv_sem.at[4, 0], to).wait_send()
            remote(
                q_ref.at[:, pl.ds(0, PAIR)], q_in.at[my_rows, :], in_send.at[t, lane, 2], q_sem.at[0], to
            ).wait_send()

    each_target(send_kv)

    def prefix_copies(p, mine):
        whose = core if mine else other
        rows = pl.ds(pl.multiple_of((2 * xp + whose) * COLUMN + p * PIECE, PIECE), PIECE)
        cols = pl.ds(pl.multiple_of(flip * HEAD_DIM, HEAD_DIM), HEAD_DIM)
        for n, src in enumerate((pk_ref, pv_ref)):
            dst = window.at[0, pl.ds(p * PIECE, PIECE), pl.ds(n * HEAD_DIM, HEAD_DIM)]
            if mine:
                yield pltpu.make_async_copy(src.at[rows, cols], dst, kv_sem.at[0, p])
            else:
                yield remote(
                    src.at[rows, cols], dst, prefix_send.at[p, n], kv_sem.at[0, p],
                    device(y, x, z, other),
                )

    has_prefix = (y == 0) & (core == z_hi)

    @pl.when(has_prefix)
    def _():
        for p in range(PIECES):
            for mine in (True, False):
                for copy in prefix_copies(p, mine):
                    copy.start()

    each_target(send_q)

    def piece_at(i):
        return (z // 2 + ring_offset(i) + 4) % 4

    def routes(slot):
        across = device(y, x, z, other)
        near = device(y, x_near, z, core)
        if slot == 4:
            return (
                (y < 3, device((y + 1) % 4, x, z, core), 0, 0),
                (xp == 0, near, 2, 1),
                (core == 0, across, 3, 2),
            )
        if slot == 0:
            return ((xp == 1, near, 2, 1), (core == 1, across, 1, 3))
        return ((core == 0, across, 1, 3), (core == 1, across, 3, 2))

    def arrived(slot, p):
        rows = pl.ds(pl.multiple_of(p * PIECE, PIECE), PIECE)
        ref = window.at[slot, rows, :]
        pltpu.make_async_copy(ref, ref, kv_sem.at[slot, p]).wait()

    def forward(slot, p, start):
        rows = pl.ds(pl.multiple_of(p * PIECE, PIECE), PIECE)
        for condition, to, there, n in routes(slot):

            @pl.when(condition)
            def _():
                copy = remote(
                    window.at[slot, rows, :], window.at[there, rows, :],
                    fwd_send.at[n, p], kv_sem.at[there, p], to,
                )
                copy.start() if start else copy.wait_send()

    order = sorted((i + d, d, slot, i) for d, slot in enumerate((4, 0, 2)) for i in range(PIECES))
    for _, _, slot, i in order:
        p = piece_at(i)
        arrived(slot, p)
        forward(slot, p, True)
    for slot in (1, 3):
        for p in range(PIECES):
            arrived(slot, p)

    first_row = WINDOW - (4 * y + my_column) * COLUMN - start_ref[0]
    spare = window[4, 0:1, 0:HEAD_DIM].astype(jnp.float32)

    def build(i, carry):
        slot, p = i // PIECES, i % PIECES
        rows = pl.ds(pl.multiple_of(p * PIECE, PIECE), PIECE)
        at = pl.ds(pl.multiple_of(i * PIECE, PIECE), PIECE)
        row = i * PIECE + lax.broadcasted_iota(jnp.int32, (PIECE, HEAD_DIM), 0)
        real = row >= first_row
        k = jnp.where(real, window[slot, rows, 0:HEAD_DIM].astype(jnp.float32), spare)
        v = jnp.where(real, window[slot, rows, HEAD_DIM:PAIR].astype(jnp.float32), 0.0)
        k = k.astype(jnp.bfloat16)
        keys2[at, 0:HEAD_DIM] = k
        keys2[at, HEAD_DIM:PAIR] = k
        values2[at, 0:HEAD_DIM] = v.astype(jnp.bfloat16)
        values2[at, HEAD_DIM:PAIR] = jnp.where(real, 1.0, 0.0).astype(jnp.bfloat16)
        return carry

    lax.fori_loop(0, SLOTS * PIECES, build, 0)

    def queries(i):
        p = piece_at(i)
        rows = pl.ds(pl.multiple_of(p * PIECE, PIECE), PIECE)
        ref = q_in.at[rows, :]
        pltpu.make_async_copy(ref, ref, q_sem.at[p]).wait()
        for h in range(2):
            scaled = q_in[rows, h * HEAD_DIM : (h + 1) * HEAD_DIM].astype(jnp.float32) * LOG2E_SCALED
            high = scaled.astype(jnp.bfloat16)
            q2[h * PIECE : (h + 1) * PIECE, 0:HEAD_DIM] = high
            q2[h * PIECE : (h + 1) * PIECE, HEAD_DIM:PAIR] = (
                scaled - high.astype(jnp.float32)
            ).astype(jnp.bfloat16)

    def score(i, slot, step, peak):
        p = piece_at(i)
        at = pl.ds(pl.multiple_of((p + step) * PIECE, PIECE), PIECE)
        s = lax.dot_general(q2[...], keys2[at, :], NT, preferred_element_type=jnp.float32)
        if step in (0, STEPS - 1):
            token = lax.broadcasted_iota(jnp.int32, s.shape, 0) % PIECE
            key = lax.broadcasted_iota(jnp.int32, s.shape, 1)
            s = jnp.where(key > token if step == 0 else key <= token, s, MASKED)
        scores[slot, :, step * PIECE : (step + 1) * PIECE] = s
        for lane in range(0, PIECE, HEAD_DIM):
            peak = jnp.maximum(peak, s[:, lane : lane + HEAD_DIM])
        return peak

    def no_peak():
        return jnp.full((2 * PIECE, HEAD_DIM), MASKED, jnp.float32)

    def keep_peak(slot, peak):
        peaks[slot] = jnp.broadcast_to(jnp.max(peak, axis=1, keepdims=True), peak.shape)

    def mix(i, slot, step):
        p = piece_at(i)
        at = pl.ds(pl.multiple_of((p + step) * PIECE, PIECE), PIECE)
        peak = peaks[slot]
        weights = [
            jnp.exp2(scores[slot, :, lane : lane + HEAD_DIM] - peak).astype(jnp.bfloat16)
            for lane in range(step * PIECE, (step + 1) * PIECE, HEAD_DIM)
        ]
        return jnp.dot(
            jnp.concatenate(weights, axis=1), values2[at, :], preferred_element_type=jnp.float32
        )

    def home_copies(i, start):
        p = piece_at(i)
        cols = pl.ds(pl.multiple_of(my_head * PAIR, PAIR), PAIR)
        for n in range(4):
            z_, core_ = 2 * p + n // 2, n % 2
            mine = (my_column == x) & (z_ == z) & (core_ == core)
            src = o_out.at[p, pl.ds(n * ROWS, ROWS), :]
            dst = out_ref.at[:, cols]

            @pl.when(mine)
            def _():
                if start:
                    pltpu.make_async_copy(src, dst, o_sem).start()

            @pl.when(jnp.logical_not(mine))
            def _():
                copy = remote(src, dst, o_send.at[p, n], o_sem, device(y, my_column, z_, core_))
                copy.start() if start else copy.wait_send()

    def finish(i, total):
        p = piece_at(i)
        o = total[:, 0:HEAD_DIM] / total[:, HEAD_DIM:PAIR]
        o_out[p, :, 0:HEAD_DIM] = o[0:PIECE].astype(jnp.bfloat16)
        o_out[p, :, HEAD_DIM:PAIR] = o[PIECE:].astype(jnp.bfloat16)
        home_copies(i, True)

    queries(0)
    peak = no_peak()
    for step in range(STEPS):
        peak = score(0, 0, step, peak)
    keep_peak(0, peak)

    def piece(i, carry):
        slot = i % 2
        queries(i + 1)
        peak = no_peak()
        total = None
        for step in range(STEPS):
            peak = score(i + 1, 1 - slot, step, peak)
            part = mix(i, slot, step)
            total = part if total is None else total + part
        keep_peak(1 - slot, peak)
        finish(i, total)
        return carry

    lax.fori_loop(0, PIECES - 1, piece, 0)
    total = None
    for step in range(STEPS):
        part = mix(PIECES - 1, (PIECES - 1) % 2, step)
        total = part if total is None else total + part
    finish(PIECES - 1, total)

    pltpu.make_async_copy(out_ref, out_ref, o_sem).wait()
    each_target(sent)

    @pl.when(has_prefix)
    def _():
        for p in range(PIECES):
            for copy in prefix_copies(p, False):
                copy.wait_send()

    for slot in (4, 0, 2):
        for p in range(PIECES):
            forward(slot, p, False)
    for i in range(PIECES):
        home_copies(i, False)


def shards(queries, keys, values, prefix_keys, prefix_values, span_start):
    anywhere = pl.BlockSpec(memory_space=pl.ANY)
    return pl.pallas_call(
        kernel,
        out_shape=jax.ShapeDtypeStruct(queries.shape, jnp.bfloat16),
        in_specs=[pl.BlockSpec(memory_space=pltpu.SMEM)] + [anywhere] * 5,
        out_specs=anywhere,
        scratch_shapes=[
            pltpu.VMEM((SLOTS, COLUMN, PAIR), jnp.bfloat16),
            pltpu.VMEM((COLUMN, PAIR), jnp.bfloat16),
            pltpu.VMEM((SLOTS * COLUMN, PAIR), jnp.bfloat16),
            pltpu.VMEM((SLOTS * COLUMN, PAIR), jnp.bfloat16),
            pltpu.VMEM((2 * PIECE, PAIR), jnp.bfloat16),
            pltpu.VMEM((2, 2 * PIECE, SPAN), jnp.float32),
            pltpu.VMEM((2, 2 * PIECE, HEAD_DIM), jnp.float32),
            pltpu.VMEM((PIECES, PIECE, PAIR), jnp.bfloat16),
            pltpu.SemaphoreType.DMA((SLOTS, PIECES)),
            pltpu.SemaphoreType.DMA((PIECES,)),
            pltpu.SemaphoreType.DMA,
            pltpu.SemaphoreType.DMA((8, 2, 3)),
            pltpu.SemaphoreType.DMA((4, PIECES)),
            pltpu.SemaphoreType.DMA((PIECES, 2)),
            pltpu.SemaphoreType.DMA((PIECES, 4)),
        ],
        compiler_params=pltpu.CompilerParams(
            collective_id=0, has_side_effects=True, vmem_limit_bytes=60 << 20
        ),
    )(span_start, queries, keys, values, prefix_keys, prefix_values)


def solution(mesh):
    placed = (
        P(("seq", "head"), None),
        P(("seq", "head"), None),
        P(("seq", "head"), None),
        P(None, "head"),
        P(None, "head"),
        P(),
    )
    return jax.shard_map(
        shards, mesh=mesh, in_specs=placed, out_specs=P(("seq", "head"), None), check_vma=False
    )
```

```python
import functools
import math

import jax
import jax.numpy as jnp
from jax import lax
from jax.experimental import pallas as pl
from jax.experimental.pallas import tpu as pltpu
from jax.sharding import PartitionSpec as P

HEAD_DIM = 128
QH = 32
KVH = 16
QSCALE = 144
WINDOW = 4096

MESH = pl.DeviceIdType.MESH
ROWS = 64
COLUMN = 1024
PIECE = 256
PIECES = COLUMN // PIECE
CHIP = 128
CHIPS = COLUMN // CHIP
SLOTS = 5
SPAN = WINDOW + PIECE
STEPS = SPAN // PIECE
PAIR = 2 * HEAD_DIM
MASKED = -1e30
LOG2E_SCALED = math.log2(math.e) * QSCALE ** (-0.5)
NT = (((1,), (1,)), ((), ()))


def ring_offset(t):
    t = (8 - t) % 8
    half = (t + 1) // 2
    return jnp.where(t % 2 == 1, half, -half)


def kernel(
    start_ref, q_ref, k_ref, v_ref, pk_ref, pv_ref, out_ref,
    window, q_in, keys2, values2, q2, scores, peaks, o_out,
    kv_sem, q_sem, o_sem, in_send, fwd_send, prefix_send, o_send,
):
    seq, head = lax.axis_index("seq"), lax.axis_index("head")
    y, x, z = seq // 8, (seq // 2) % 4, (seq % 2) * 4 + head // 2
    core = head % 2
    z_hi = seq % 2
    xp, xl = x // 2, x % 2
    other = 1 - core
    my_column = 2 * xp + core
    flip = (xl + xp) % 2

    def device(y_, x_, z_, core_):
        return (y_ * 8 + x_ * 2 + z_ // 4, (z_ % 4) * 2 + core_)

    def chip_head(x_, z_):
        return (z_ % 4) * 4 + (z_ // 4) * 2 + (x_ % 2 + x_ // 2) % 2

    my_head = chip_head(x, z)
    x_near = 3 - x

    def remote(src, dst, send, recv, to):
        return pltpu.make_async_remote_copy(
            src_ref=src, dst_ref=dst, send_sem=send, recv_sem=recv,
            device_id=to, device_id_type=MESH,
        )

    barrier = pltpu.get_barrier_semaphore()

    def greet(to):
        pl.semaphore_signal(barrier, inc=1, device_id=to, device_id_type=MESH)

    def greet_group(i, carry):
        x_, z_, core_ = 2 * xp + i // 16, (i // 2) % 8, i % 2
        pl.when(jnp.logical_not((x_ == x) & (z_ == z) & (core_ == core)))(
            lambda: greet(device(y, x_, z_, core_))
        )
        return carry

    lax.fori_loop(0, 32, greet_group, 0)
    greet(device(y, x_near, z, core))
    greet(device((y + 1) % 4, x, z, core))
    greet(device((y + 3) % 4, x, z, core))
    values2[:, HEAD_DIM:PAIR] = jnp.ones((SLOTS * COLUMN, HEAD_DIM), jnp.bfloat16)
    pl.semaphore_wait(barrier, 34)

    my_rows = pl.ds(pl.multiple_of((z * 2 + core) * ROWS, ROWS), ROWS)

    def each_target(body):
        def at(t, carry):
            z_ = (z + ring_offset(t) + 8) % 8
            for lane in range(2):
                x_ = 2 * xp + lane
                mine = (t == 0) & (xl == lane) & (core == xl)
                body(t, lane, x_, z_, mine)
            return carry

        lax.fori_loop(0, 8, at, 0)

    def send_kv(t, lane, x_, z_, mine):
        h = chip_head(x_, z_)
        cols = pl.ds(pl.multiple_of(h * HEAD_DIM, HEAD_DIM), HEAD_DIM)
        for n, src in enumerate((k_ref, v_ref)):
            dst = window.at[4, my_rows, pl.ds(n * HEAD_DIM, HEAD_DIM)]
            recv = kv_sem.at[4, z]

            @pl.when(mine)
            def _():
                pltpu.make_async_copy(src.at[:, cols], dst, recv).start()

            @pl.when(jnp.logical_not(mine))
            def _():
                remote(
                    src.at[:, cols], dst, in_send.at[t, lane, n], recv, device(y, x_, z_, xl)
                ).start()

    def send_q(t, lane, x_, z_, mine):
        h = chip_head(x_, z_)
        cols = pl.ds(pl.multiple_of(h * PAIR, PAIR), PAIR)
        dst = q_in.at[my_rows, :]
        recv = q_sem.at[z // 2]

        @pl.when(mine)
        def _():
            pltpu.make_async_copy(q_ref.at[:, cols], dst, recv).start()

        @pl.when(jnp.logical_not(mine))
        def _():
            remote(
                q_ref.at[:, cols], dst, in_send.at[t, lane, 2], recv, device(y, x_, z_, xl)
            ).start()

    def sent(t, lane, x_, z_, mine):
        @pl.when(jnp.logical_not(mine))
        def _():
            to = device(y, x_, z_, xl)
            for n, src in enumerate((k_ref, v_ref)):
                cols = pl.ds(0, HEAD_DIM)
                dst = window.at[4, my_rows, pl.ds(n * HEAD_DIM, HEAD_DIM)]
                remote(src.at[:, cols], dst, in_send.at[t, lane, n], kv_sem.at[4, 0], to).wait_send()
            remote(
                q_ref.at[:, pl.ds(0, PAIR)], q_in.at[my_rows, :], in_send.at[t, lane, 2], q_sem.at[0], to
            ).wait_send()

    each_target(send_kv)

    def prefix_copies(p, mine):
        whose = core if mine else other
        rows = pl.ds(pl.multiple_of((2 * xp + whose) * COLUMN + p * CHIP, CHIP), CHIP)
        cols = pl.ds(pl.multiple_of(flip * HEAD_DIM, HEAD_DIM), HEAD_DIM)
        for n, src in enumerate((pk_ref, pv_ref)):
            dst = window.at[0, pl.ds(p * CHIP, CHIP), pl.ds(n * HEAD_DIM, HEAD_DIM)]
            if mine:
                yield pltpu.make_async_copy(src.at[rows, cols], dst, kv_sem.at[0, p])
            else:
                yield remote(
                    src.at[rows, cols], dst, prefix_send.at[p, n], kv_sem.at[0, p],
                    device(y, x, z, other),
                )

    has_prefix = (y == 0) & (core == z_hi)

    @pl.when(has_prefix)
    def _():
        for p in range(CHIPS):
            for mine in (True, False):
                for copy in prefix_copies(p, mine):
                    copy.start()

    each_target(send_q)

    toward = jnp.where(z % 2 == 0, 1, 3)

    def piece_at(i):
        return (z // 2 + jnp.where(i == 0, 2, jnp.where(i == 1, toward, jnp.where(i == 2, -toward, 0))) + 4) % 4

    def routes(slot):
        across = device(y, x, z, other)
        near = device(y, x_near, z, core)
        if slot == 4:
            return (
                (y < 3, device((y + 1) % 4, x, z, core), 0, 0),
                (xp == 0, near, 2, 1),
                (core == 0, across, 3, 2),
            )
        if slot == 0:
            return ((xp == 1, near, 2, 1), (core == 1, across, 1, 3))
        return ((core == 0, across, 1, 3), (core == 1, across, 3, 2))

    def arrived(slot, p):
        rows = pl.ds(pl.multiple_of(p * CHIP, CHIP), CHIP)
        ref = window.at[slot, rows, :]
        pltpu.make_async_copy(ref, ref, kv_sem.at[slot, p]).wait()

    def forward(slot, p, start):
        rows = pl.ds(pl.multiple_of(p * CHIP, CHIP), CHIP)
        for condition, to, there, n in routes(slot):

            @pl.when(condition)
            def _():
                copy = remote(
                    window.at[slot, rows, :], window.at[there, rows, :],
                    fwd_send.at[n, p], kv_sem.at[there, p], to,
                )
                copy.start() if start else copy.wait_send()

    def build(slot, p):
        rows = pl.ds(pl.multiple_of(p * CHIP, CHIP), CHIP)
        at = pl.ds(pl.multiple_of(slot * COLUMN + p * CHIP, CHIP), CHIP)
        k = window[slot, rows, 0:HEAD_DIM]
        keys2[at, 0:HEAD_DIM] = k
        keys2[at, HEAD_DIM:PAIR] = k
        values2[at, 0:HEAD_DIM] = window[slot, rows, HEAD_DIM:PAIR]

    def relay(i, carry):
        for lag, slot in ((0, 4), (2, 0), (4, 2)):

            @pl.when((i >= lag) & (i < lag + CHIPS))
            def _():
                p = (z - ring_offset(i - lag) + 8) % 8
                arrived(slot, p)
                forward(slot, p, True)
                build(slot, p)

        return carry

    lax.fori_loop(0, CHIPS + 4, relay, 0)

    def last(i, carry):
        for slot in (3, 1):
            p = (z - ring_offset(i) + 8) % 8
            arrived(slot, p)
            build(slot, p)
        return carry

    lax.fori_loop(0, CHIPS, last, 0)

    @pl.when(y == 0)
    def _():
        first_row = WINDOW - my_column * COLUMN - start_ref[0]
        spare = window[4, 0:1, 0:HEAD_DIM].astype(jnp.float32)

        def fix(i, carry):
            at = pl.ds(pl.multiple_of(i * PIECE, PIECE), PIECE)
            real = i * PIECE + lax.broadcasted_iota(jnp.int32, (PIECE, HEAD_DIM), 0) >= first_row
            k = jnp.where(real, keys2[at, 0:HEAD_DIM].astype(jnp.float32), spare).astype(jnp.bfloat16)
            v = jnp.where(real, values2[at, 0:HEAD_DIM].astype(jnp.float32), 0.0)
            keys2[at, 0:HEAD_DIM] = k
            keys2[at, HEAD_DIM:PAIR] = k
            values2[at, 0:HEAD_DIM] = v.astype(jnp.bfloat16)
            values2[at, HEAD_DIM:PAIR] = jnp.where(real, 1.0, 0.0).astype(jnp.bfloat16)
            return carry

        lax.fori_loop(0, WINDOW // PIECE, fix, 0)

    def queries(i):
        p = piece_at(i)
        rows = pl.ds(pl.multiple_of(p * PIECE, PIECE), PIECE)
        ref = q_in.at[rows, :]
        pltpu.make_async_copy(ref, ref, q_sem.at[p]).wait()
        for h in range(2):
            scaled = q_in[rows, h * HEAD_DIM : (h + 1) * HEAD_DIM].astype(jnp.float32) * LOG2E_SCALED
            high = scaled.astype(jnp.bfloat16)
            q2[h * PIECE : (h + 1) * PIECE, 0:HEAD_DIM] = high
            q2[h * PIECE : (h + 1) * PIECE, HEAD_DIM:PAIR] = (
                scaled - high.astype(jnp.float32)
            ).astype(jnp.bfloat16)

    def score(i, slot, step, peak):
        p = piece_at(i)
        at = pl.ds(pl.multiple_of((p + step) * PIECE, PIECE), PIECE)
        s = lax.dot_general(q2[...], keys2[at, :], NT, preferred_element_type=jnp.float32)
        if step in (0, STEPS - 1):
            token = lax.broadcasted_iota(jnp.int32, s.shape, 0) % PIECE
            key = lax.broadcasted_iota(jnp.int32, s.shape, 1)
            s = jnp.where(key > token if step == 0 else key <= token, s, MASKED)
        scores[slot, :, step * PIECE : (step + 1) * PIECE] = s
        for lane in range(0, PIECE, HEAD_DIM):
            peak = jnp.maximum(peak, s[:, lane : lane + HEAD_DIM])
        return peak

    def no_peak():
        return jnp.full((2 * PIECE, HEAD_DIM), MASKED, jnp.float32)

    def keep_peak(slot, peak):
        peaks[slot] = jnp.broadcast_to(jnp.max(peak, axis=1, keepdims=True), peak.shape)

    def mix(i, slot, step):
        p = piece_at(i)
        at = pl.ds(pl.multiple_of((p + step) * PIECE, PIECE), PIECE)
        peak = peaks[slot]
        weights = [
            jnp.exp2(scores[slot, :, lane : lane + HEAD_DIM] - peak).astype(jnp.bfloat16)
            for lane in range(step * PIECE, (step + 1) * PIECE, HEAD_DIM)
        ]
        return jnp.dot(
            jnp.concatenate(weights, axis=1), values2[at, :], preferred_element_type=jnp.float32
        )

    def home_copies(i, start):
        p = piece_at(i)
        cols = pl.ds(pl.multiple_of(my_head * PAIR, PAIR), PAIR)
        for n in range(4):
            z_, core_ = 2 * p + n // 2, n % 2
            mine = (my_column == x) & (z_ == z) & (core_ == core)
            src = o_out.at[p, pl.ds(n * ROWS, ROWS), :]
            dst = out_ref.at[:, cols]

            @pl.when(mine)
            def _():
                if start:
                    pltpu.make_async_copy(src, dst, o_sem).start()

            @pl.when(jnp.logical_not(mine))
            def _():
                copy = remote(src, dst, o_send.at[p, n], o_sem, device(y, my_column, z_, core_))
                copy.start() if start else copy.wait_send()

    def finish(i, total):
        p = piece_at(i)
        o = total[:, 0:HEAD_DIM] / total[:, HEAD_DIM:PAIR]
        o_out[p, :, 0:HEAD_DIM] = o[0:PIECE].astype(jnp.bfloat16)
        o_out[p, :, HEAD_DIM:PAIR] = o[PIECE:].astype(jnp.bfloat16)
        home_copies(i, True)

    queries(0)
    peak = no_peak()
    for step in range(STEPS):
        peak = score(0, 0, step, peak)
    keep_peak(0, peak)

    def piece(i, carry):
        slot = i % 2
        queries(i + 1)
        peak = no_peak()
        total = None
        for step in range(STEPS):
            peak = score(i + 1, 1 - slot, step, peak)
            part = mix(i, slot, step)
            total = part if total is None else total + part
        keep_peak(1 - slot, peak)
        finish(i, total)
        return carry

    lax.fori_loop(0, PIECES - 1, piece, 0)
    total = None
    for step in range(STEPS):
        part = mix(PIECES - 1, (PIECES - 1) % 2, step)
        total = part if total is None else total + part
    finish(PIECES - 1, total)

    pltpu.make_async_copy(out_ref, out_ref, o_sem).wait()
    each_target(sent)

    @pl.when(has_prefix)
    def _():
        for p in range(CHIPS):
            for copy in prefix_copies(p, False):
                copy.wait_send()

    def forwarded(p, carry):
        for slot in (4, 0, 2):
            forward(slot, p, False)
        return carry

    lax.fori_loop(0, CHIPS, forwarded, 0)
    for i in range(PIECES):
        home_copies(i, False)


def shards(queries, keys, values, prefix_keys, prefix_values, span_start):
    anywhere = pl.BlockSpec(memory_space=pl.ANY)
    return pl.pallas_call(
        kernel,
        out_shape=jax.ShapeDtypeStruct(queries.shape, jnp.bfloat16),
        in_specs=[pl.BlockSpec(memory_space=pltpu.SMEM)] + [anywhere] * 5,
        out_specs=anywhere,
        scratch_shapes=[
            pltpu.VMEM((SLOTS, COLUMN, PAIR), jnp.bfloat16),
            pltpu.VMEM((COLUMN, PAIR), jnp.bfloat16),
            pltpu.VMEM((SLOTS * COLUMN, PAIR), jnp.bfloat16),
            pltpu.VMEM((SLOTS * COLUMN, PAIR), jnp.bfloat16),
            pltpu.VMEM((2 * PIECE, PAIR), jnp.bfloat16),
            pltpu.VMEM((2, 2 * PIECE, SPAN), jnp.float32),
            pltpu.VMEM((2, 2 * PIECE, HEAD_DIM), jnp.float32),
            pltpu.VMEM((PIECES, PIECE, PAIR), jnp.bfloat16),
            pltpu.SemaphoreType.DMA((SLOTS, CHIPS)),
            pltpu.SemaphoreType.DMA((PIECES,)),
            pltpu.SemaphoreType.DMA,
            pltpu.SemaphoreType.DMA((8, 2, 3)),
            pltpu.SemaphoreType.DMA((4, CHIPS)),
            pltpu.SemaphoreType.DMA((CHIPS, 2)),
            pltpu.SemaphoreType.DMA((PIECES, 4)),
        ],
        compiler_params=pltpu.CompilerParams(
            collective_id=0, has_side_effects=True, vmem_limit_bytes=60 << 20
        ),
    )(span_start, queries, keys, values, prefix_keys, prefix_values)


def solution(mesh):
    placed = (
        P(("seq", "head"), None),
        P(("seq", "head"), None),
        P(("seq", "head"), None),
        P(None, "head"),
        P(None, "head"),
        P(),
    )
    return jax.shard_map(
        shards, mesh=mesh, in_specs=placed, out_specs=P(("seq", "head"), None), check_vma=False
    )
```

```python
import functools
import math

import jax
import jax.numpy as jnp
from jax import lax
from jax.experimental import pallas as pl
from jax.experimental.pallas import tpu as pltpu
from jax.sharding import PartitionSpec as P

HEAD_DIM = 128
QH = 32
KVH = 16
QSCALE = 144
WINDOW = 4096

LOGICAL = pl.DeviceIdType.LOGICAL
ROWS = 64
COLUMN = 1024
PIECE = 256
PIECES = COLUMN // PIECE
CHIP = 128
CHIPS = COLUMN // CHIP
AHEAD = 8
SLOTS = 5
SPAN = WINDOW + PIECE
STEPS = SPAN // PIECE
PAIR = 2 * HEAD_DIM
MASKED = -1e30
LOG2E_SCALED = math.log2(math.e) * QSCALE ** (-0.5)
NT = (((1,), (1,)), ((), ()))


def ring_offset(t):
    half = (t + 1) // 2
    return jnp.where(t % 2 == 1, half, -half)


def kernel(
    start_ref, q_ref, k_ref, v_ref, pk_ref, pv_ref, out_ref,
    window, q_in, keys2, values2, q2, even_scores, odd_scores, even_peaks, odd_peaks, o_out,
    kv_sem, q_sem, o_sem, in_send, fwd_send, prefix_send, o_send,
):
    seq, head = lax.axis_index("seq"), lax.axis_index("head")
    y, x, z = seq // 8, (seq // 2) % 4, (seq % 2) * 4 + head // 2
    core = head % 2
    z_hi = seq % 2
    xp, xl = x // 2, x % 2
    other = 1 - core
    my_column = 2 * xp + core
    flip = (xl + xp) % 2

    def device(y_, x_, z_, core_):
        return y_ * 64 + x_ * 16 + z_ * 2 + core_

    def chip_head(x_, z_):
        return (z_ % 4) * 4 + (z_ // 4) * 2 + (x_ % 2 + x_ // 2) % 2

    my_head = chip_head(x, z)
    x_near = 3 - x

    def remote(src, dst, send, recv, to):
        return pltpu.make_async_remote_copy(
            src_ref=src, dst_ref=dst, send_sem=send, recv_sem=recv,
            device_id=to, device_id_type=LOGICAL,
        )

    barrier = pltpu.get_barrier_semaphore()

    def greet(to):
        pl.semaphore_signal(barrier, inc=1, device_id=to, device_id_type=LOGICAL)

    group = device(y, 2 * xp, 0, 0)
    place = device(0, xl, z, core)
    for i in range(16, 48):
        if i != 32:
            greet(group + lax.rem(place + i, 32))
    greet(device(y, x_near, z, core))
    greet(device((y + 1) % 4, x, z, core))
    greet(device((y + 3) % 4, x, z, core))
    values2[:, HEAD_DIM:PAIR] = jnp.ones((SLOTS * COLUMN, HEAD_DIM), jnp.bfloat16)
    pl.semaphore_wait(barrier, 34)

    my_rows = pl.ds(pl.multiple_of((z * 2 + core) * ROWS, ROWS), ROWS)

    def targets(body, t):
        z_ = (z + ring_offset(t) + 8) % 8
        for lane in range(2):
            x_ = 2 * xp + lane
            mine = (t == 0) & (xl == lane) & (core == xl)
            body(t, lane, x_, z_, mine)

    def each_target(body, first=0, stop=8):
        def at(t, carry):
            targets(body, t)
            return carry

        lax.fori_loop(first, stop, at, 0)

    def send_kv(t, lane, x_, z_, mine):
        h = chip_head(x_, z_)
        cols = pl.ds(pl.multiple_of(h * HEAD_DIM, HEAD_DIM), HEAD_DIM)
        for n, src in enumerate((k_ref, v_ref)):
            dst = window.at[4, my_rows, pl.ds(n * HEAD_DIM, HEAD_DIM)]
            recv = kv_sem.at[4, z]

            @pl.when(mine)
            def _():
                pltpu.make_async_copy(src.at[:, cols], dst, recv).start()

            @pl.when(jnp.logical_not(mine))
            def _():
                remote(
                    src.at[:, cols], dst, in_send.at[t, lane, n], recv, device(y, x_, z_, xl)
                ).start()

    def send_q(t, lane, x_, z_, mine):
        h = chip_head(x_, z_)
        cols = pl.ds(pl.multiple_of(h * PAIR, PAIR), PAIR)
        dst = q_in.at[my_rows, :]
        recv = q_sem.at[z // 2]

        @pl.when(mine)
        def _():
            pltpu.make_async_copy(q_ref.at[:, cols], dst, recv).start()

        @pl.when(jnp.logical_not(mine))
        def _():
            remote(
                q_ref.at[:, cols], dst, in_send.at[t, lane, 2], recv, device(y, x_, z_, xl)
            ).start()

    def sent(t, lane, x_, z_, mine):
        @pl.when(jnp.logical_not(mine))
        def _():
            to = device(y, x_, z_, xl)
            for n, src in enumerate((k_ref, v_ref)):
                cols = pl.ds(0, HEAD_DIM)
                dst = window.at[4, my_rows, pl.ds(n * HEAD_DIM, HEAD_DIM)]
                remote(src.at[:, cols], dst, in_send.at[t, lane, n], kv_sem.at[4, 0], to).wait_send()
            remote(
                q_ref.at[:, pl.ds(0, PAIR)], q_in.at[my_rows, :], in_send.at[t, lane, 2], q_sem.at[0], to
            ).wait_send()

    each_target(send_kv, 0, AHEAD)

    def prefix_copies(p, mine):
        whose = core if mine else other
        rows = pl.ds(pl.multiple_of((2 * xp + whose) * COLUMN + p * CHIP, CHIP), CHIP)
        cols = pl.ds(pl.multiple_of(flip * HEAD_DIM, HEAD_DIM), HEAD_DIM)
        for n, src in enumerate((pk_ref, pv_ref)):
            dst = window.at[0, pl.ds(p * CHIP, CHIP), pl.ds(n * HEAD_DIM, HEAD_DIM)]
            if mine:
                yield pltpu.make_async_copy(src.at[rows, cols], dst, kv_sem.at[0, p])
            else:
                yield remote(
                    src.at[rows, cols], dst, prefix_send.at[p, n], kv_sem.at[0, p],
                    device(y, x, z, other),
                )

    has_prefix = (y == 0) & (core == z_hi)

    @pl.when(has_prefix)
    def _():
        for p in range(CHIPS):
            for mine in (True, False):
                for copy in prefix_copies(p, mine):
                    copy.start()

    toward = jnp.where(z % 2 == 0, 1, 3)

    def piece_at(i):
        return (z // 2 + jnp.where(i == 0, 2, jnp.where(i == 1, toward, jnp.where(i == 2, -toward, 0))) + 4) % 4

    def routes(slot):
        across = device(y, x, z, other)
        near = device(y, x_near, z, core)
        if slot == 4:
            return (
                (y < 3, device((y + 1) % 4, x, z, core), 0, 0),
                (xp == 0, near, 2, 1),
                (core == 0, across, 3, 2),
            )
        if slot == 0:
            return ((xp == 1, near, 2, 1), (core == 1, across, 1, 3))
        return ((core == 0, across, 1, 3), (core == 1, across, 3, 2))

    def arrived(slot, p):
        rows = pl.ds(pl.multiple_of(p * CHIP, CHIP), CHIP)
        ref = window.at[slot, rows, :]
        pltpu.make_async_copy(ref, ref, kv_sem.at[slot, p]).wait()

    def forward(slot, p, start):
        rows = pl.ds(pl.multiple_of(p * CHIP, CHIP), CHIP)
        for condition, to, there, n in routes(slot):

            @pl.when(condition)
            def _():
                copy = remote(
                    window.at[slot, rows, :], window.at[there, rows, :],
                    fwd_send.at[n, p], kv_sem.at[there, p], to,
                )
                copy.start() if start else copy.wait_send()

    def build(slot, p):
        rows = pl.ds(pl.multiple_of(p * CHIP, CHIP), CHIP)
        at = pl.ds(pl.multiple_of(slot * COLUMN + p * CHIP, CHIP), CHIP)
        k = window[slot, rows, 0:HEAD_DIM]
        keys2[at, 0:HEAD_DIM] = k
        keys2[at, HEAD_DIM:PAIR] = k
        values2[at, 0:HEAD_DIM] = window[slot, rows, HEAD_DIM:PAIR]

    def relay(i, carry):
        for lag, slot in ((0, 4), (2, 0), (4, 2)):

            @pl.when((i >= lag) & (i < lag + CHIPS))
            def _():
                p = (z - ring_offset(i - lag) + 8) % 8
                arrived(slot, p)
                forward(slot, p, True)
                build(slot, p)
            if slot == 4:
                pl.when(i + AHEAD < 8)(lambda: targets(send_kv, i + AHEAD))
                pl.when((i + AHEAD >= 8) & (i + AHEAD < 16))(lambda: targets(send_q, i + AHEAD - 8))

        return carry

    lax.fori_loop(0, CHIPS + 5, relay, 0)

    def last(i, carry):
        for slot in (3, 1):
            p = (z - ring_offset(i) + 8) % 8
            arrived(slot, p)
            build(slot, p)
        return carry

    lax.fori_loop(0, CHIPS, last, 0)

    @pl.when(y == 0)
    def _():
        first_row = WINDOW - my_column * COLUMN - start_ref[0]
        spare = window[4, 0:1, 0:HEAD_DIM].astype(jnp.float32)

        def fix(i, carry):
            at = pl.ds(pl.multiple_of(i * PIECE, PIECE), PIECE)
            real = i * PIECE + lax.broadcasted_iota(jnp.int32, (PIECE, HEAD_DIM), 0) >= first_row
            k = jnp.where(real, keys2[at, 0:HEAD_DIM].astype(jnp.float32), spare).astype(jnp.bfloat16)
            v = jnp.where(real, values2[at, 0:HEAD_DIM].astype(jnp.float32), 0.0)
            keys2[at, 0:HEAD_DIM] = k
            keys2[at, HEAD_DIM:PAIR] = k
            values2[at, 0:HEAD_DIM] = v.astype(jnp.bfloat16)
            values2[at, HEAD_DIM:PAIR] = jnp.where(real, 1.0, 0.0).astype(jnp.bfloat16)
            return carry

        lax.fori_loop(0, WINDOW // PIECE, fix, 0)

    scores = (even_scores, odd_scores)
    peaks = (even_peaks, odd_peaks)

    def queries(i):
        p = piece_at(i)
        rows = pl.ds(pl.multiple_of(p * PIECE, PIECE), PIECE)
        ref = q_in.at[rows, :]
        pltpu.make_async_copy(ref, ref, q_sem.at[p]).wait()
        for h in range(2):
            scaled = q_in[rows, h * HEAD_DIM : (h + 1) * HEAD_DIM].astype(jnp.float32) * LOG2E_SCALED
            high = scaled.astype(jnp.bfloat16)
            q2[h * PIECE : (h + 1) * PIECE, 0:HEAD_DIM] = high
            q2[h * PIECE : (h + 1) * PIECE, HEAD_DIM:PAIR] = (
                scaled - high.astype(jnp.float32)
            ).astype(jnp.bfloat16)

    def score(i, slot, step, peak):
        p = piece_at(i)
        at = pl.ds(pl.multiple_of((p + step) * PIECE, PIECE), PIECE)
        s = lax.dot_general(q2[...], keys2[at, :], NT, preferred_element_type=jnp.float32)
        if step in (0, STEPS - 1):
            token = lax.broadcasted_iota(jnp.int32, s.shape, 0) % PIECE
            key = lax.broadcasted_iota(jnp.int32, s.shape, 1)
            s = jnp.where(key > token if step == 0 else key <= token, s, MASKED)
        scores[slot][:, step * PIECE : (step + 1) * PIECE] = s
        for lane in range(0, PIECE, HEAD_DIM):
            peak = jnp.maximum(peak, s[:, lane : lane + HEAD_DIM])
        return peak

    def no_peak():
        return jnp.full((2 * PIECE, HEAD_DIM), MASKED, jnp.float32)

    def keep_peak(slot, peak):
        peaks[slot][...] = jnp.broadcast_to(jnp.max(peak, axis=1, keepdims=True), peak.shape)

    def mix(i, slot, step):
        p = piece_at(i)
        at = pl.ds(pl.multiple_of((p + step) * PIECE, PIECE), PIECE)
        peak = peaks[slot][...]
        weights = [
            jnp.exp2(scores[slot][:, lane : lane + HEAD_DIM] - peak).astype(jnp.bfloat16)
            for lane in range(step * PIECE, (step + 1) * PIECE, HEAD_DIM)
        ]
        return jnp.dot(
            jnp.concatenate(weights, axis=1), values2[at, :], preferred_element_type=jnp.float32
        )

    def home_copies(i, start):
        p = piece_at(i)
        cols = pl.ds(pl.multiple_of(my_head * PAIR, PAIR), PAIR)
        for n in range(4):
            z_, core_ = 2 * p + n // 2, n % 2
            mine = (my_column == x) & (z_ == z) & (core_ == core)
            src = o_out.at[p, pl.ds(n * ROWS, ROWS), :]
            dst = out_ref.at[:, cols]

            @pl.when(mine)
            def _():
                if start:
                    pltpu.make_async_copy(src, dst, o_sem).start()

            @pl.when(jnp.logical_not(mine))
            def _():
                copy = remote(src, dst, o_send.at[p, n], o_sem, device(y, my_column, z_, core_))
                copy.start() if start else copy.wait_send()

    def finish(i, total):
        p = piece_at(i)
        o = total[:, 0:HEAD_DIM] / total[:, HEAD_DIM:PAIR]
        o_out[p, :, 0:HEAD_DIM] = o[0:PIECE].astype(jnp.bfloat16)
        o_out[p, :, HEAD_DIM:PAIR] = o[PIECE:].astype(jnp.bfloat16)
        home_copies(i, True)

    queries(0)
    peak = no_peak()
    for step in range(STEPS):
        peak = score(0, 0, step, peak)
    keep_peak(0, peak)

    for i in range(PIECES - 1):
        slot = i % 2
        queries(i + 1)
        peak = no_peak()
        total = None
        for step in range(STEPS):
            peak = score(i + 1, 1 - slot, step, peak)
            part = mix(i, slot, step)
            total = part if total is None else total + part
        keep_peak(1 - slot, peak)
        finish(i, total)

    total = None
    for step in range(STEPS):
        part = mix(PIECES - 1, (PIECES - 1) % 2, step)
        total = part if total is None else total + part
    finish(PIECES - 1, total)

    pltpu.make_async_copy(out_ref, out_ref, o_sem).wait()
    each_target(sent)

    @pl.when(has_prefix)
    def _():
        for p in range(CHIPS):
            for copy in prefix_copies(p, False):
                copy.wait_send()

    def forwarded(p, carry):
        for slot in (4, 0, 2):
            forward(slot, p, False)
        return carry

    lax.fori_loop(0, CHIPS, forwarded, 0)
    for i in range(PIECES):
        home_copies(i, False)


def shards(queries, keys, values, prefix_keys, prefix_values, span_start):
    anywhere = pl.BlockSpec(memory_space=pl.ANY)
    return pl.pallas_call(
        kernel,
        out_shape=pltpu.VMEM(queries.shape, jnp.bfloat16),
        in_specs=[pl.BlockSpec(memory_space=pltpu.SMEM)] + [anywhere] * 5,
        out_specs=pl.BlockSpec(memory_space=pltpu.VMEM),
        scratch_shapes=[
            pltpu.VMEM((SLOTS, COLUMN, PAIR), jnp.bfloat16),
            pltpu.VMEM((COLUMN, PAIR), jnp.bfloat16),
            pltpu.VMEM((SLOTS * COLUMN, PAIR), jnp.bfloat16),
            pltpu.VMEM((SLOTS * COLUMN, PAIR), jnp.bfloat16),
            pltpu.VMEM((2 * PIECE, PAIR), jnp.bfloat16),
            pltpu.VMEM((2 * PIECE, SPAN), jnp.float32),
            pltpu.VMEM((2 * PIECE, SPAN), jnp.float32),
            pltpu.VMEM((2 * PIECE, HEAD_DIM), jnp.float32),
            pltpu.VMEM((2 * PIECE, HEAD_DIM), jnp.float32),
            pltpu.VMEM((PIECES, PIECE, PAIR), jnp.bfloat16),
            pltpu.SemaphoreType.DMA((SLOTS, CHIPS)),
            pltpu.SemaphoreType.DMA((PIECES,)),
            pltpu.SemaphoreType.DMA,
            pltpu.SemaphoreType.DMA((8, 2, 3)),
            pltpu.SemaphoreType.DMA((4, CHIPS)),
            pltpu.SemaphoreType.DMA((CHIPS, 2)),
            pltpu.SemaphoreType.DMA((PIECES, 4)),
        ],
        compiler_params=pltpu.CompilerParams(
            collective_id=0, has_side_effects=True, vmem_limit_bytes=60 << 20
        ),
    )(span_start, queries, keys, values, prefix_keys, prefix_values)


def solution(mesh):
    placed = (
        P(("seq", "head"), None),
        P(("seq", "head"), None),
        P(("seq", "head"), None),
        P(None, "head"),
        P(None, "head"),
        P(),
    )
    return jax.shard_map(
        shards, mesh=mesh, in_specs=placed, out_specs=P(("seq", "head"), None), check_vma=False
    )
```

```python
import functools
import math

import jax
import jax.numpy as jnp
from jax import lax
from jax.experimental import pallas as pl
from jax.experimental.pallas import tpu as pltpu
from jax.sharding import PartitionSpec as P

HEAD_DIM = 128
QH = 32
KVH = 16
QSCALE = 144
WINDOW = 4096

LOGICAL = pl.DeviceIdType.LOGICAL
ROWS = 64
COLUMN = 1024
PIECE = 256
PIECES = COLUMN // PIECE
CHIP = 128
CHIPS = COLUMN // CHIP
AHEAD = 6
SLOTS = 5
SPAN = WINDOW + PIECE
STEPS = SPAN // PIECE
PAIR = 2 * HEAD_DIM
MASKED = -1e30
LOG2E_SCALED = math.log2(math.e) * QSCALE ** (-0.5)
NT = (((1,), (1,)), ((), ()))


def ring_offset(t):
    half = (t + 1) // 2
    return jnp.where(t % 2 == 1, half, -half)


def kernel(
    start_ref, q_ref, k_ref, v_ref, pk_ref, pv_ref, out_ref,
    window, q_in, keys2, values2, q2, even_scores, odd_scores, even_peaks, odd_peaks, o_out,
    kv_sem, q_sem, o_sem, in_send, fwd_send, prefix_send, o_send,
):
    seq, head = lax.axis_index("seq"), lax.axis_index("head")
    y, x, z = seq // 8, (seq // 2) % 4, (seq % 2) * 4 + head // 2
    core = head % 2
    z_hi = seq % 2
    xp, xl = x // 2, x % 2
    other = 1 - core
    my_column = 2 * xp + core
    flip = (xl + xp) % 2

    def device(y_, x_, z_, core_):
        return y_ * 64 + x_ * 16 + z_ * 2 + core_

    def chip_head(x_, z_):
        return (z_ % 4) * 4 + (z_ // 4) * 2 + (x_ % 2 + x_ // 2) % 2

    my_head = chip_head(x, z)
    x_near = 3 - x

    def remote(src, dst, send, recv, to):
        return pltpu.make_async_remote_copy(
            src_ref=src, dst_ref=dst, send_sem=send, recv_sem=recv,
            device_id=to, device_id_type=LOGICAL,
        )

    barrier = pltpu.get_barrier_semaphore()

    def greet(to):
        pl.semaphore_signal(barrier, inc=1, device_id=to, device_id_type=LOGICAL)

    group = device(y, 2 * xp, 0, 0)
    place = device(0, xl, z, core)
    for i in range(16, 48):
        if i != 32:
            greet(group + lax.rem(place + i, 32))
    greet(device(y, x_near, z, core))
    greet(device((y + 1) % 4, x, z, core))
    greet(device((y + 3) % 4, x, z, core))
    values2[:, HEAD_DIM:PAIR] = jnp.ones((SLOTS * COLUMN, HEAD_DIM), jnp.bfloat16)
    pl.semaphore_wait(barrier, 34)

    my_rows = pl.ds(pl.multiple_of((z * 2 + core) * ROWS, ROWS), ROWS)

    def targets(body, t):
        z_ = (z + ring_offset(t) + 8) % 8
        for lane in range(2):
            x_ = 2 * xp + lane
            mine = (t == 0) & (xl == lane) & (core == xl)
            body(t, lane, x_, z_, mine)

    def each_target(body, first=0, stop=8):
        def at(t, carry):
            targets(body, t)
            return carry

        lax.fori_loop(first, stop, at, 0)

    def send_kv(t, lane, x_, z_, mine):
        h = chip_head(x_, z_)
        cols = pl.ds(pl.multiple_of(h * HEAD_DIM, HEAD_DIM), HEAD_DIM)
        for n, src in enumerate((k_ref, v_ref)):
            dst = window.at[4, my_rows, pl.ds(n * HEAD_DIM, HEAD_DIM)]
            recv = kv_sem.at[4, z]

            @pl.when(mine)
            def _():
                pltpu.make_async_copy(src.at[:, cols], dst, recv).start()

            @pl.when(jnp.logical_not(mine))
            def _():
                remote(
                    src.at[:, cols], dst, in_send.at[t, lane, n], recv, device(y, x_, z_, xl)
                ).start()

    def send_q(t, lane, x_, z_, mine):
        h = chip_head(x_, z_)
        cols = pl.ds(pl.multiple_of(h * PAIR, PAIR), PAIR)
        dst = q_in.at[my_rows, :]
        recv = q_sem.at[z // 2]

        @pl.when(mine)
        def _():
            pltpu.make_async_copy(q_ref.at[:, cols], dst, recv).start()

        @pl.when(jnp.logical_not(mine))
        def _():
            remote(
                q_ref.at[:, cols], dst, in_send.at[t, lane, 2], recv, device(y, x_, z_, xl)
            ).start()

    def sent(t, lane, x_, z_, mine):
        @pl.when(jnp.logical_not(mine))
        def _():
            to = device(y, x_, z_, xl)
            for n, src in enumerate((k_ref, v_ref)):
                cols = pl.ds(0, HEAD_DIM)
                dst = window.at[4, my_rows, pl.ds(n * HEAD_DIM, HEAD_DIM)]
                remote(src.at[:, cols], dst, in_send.at[t, lane, n], kv_sem.at[4, 0], to).wait_send()
            remote(
                q_ref.at[:, pl.ds(0, PAIR)], q_in.at[my_rows, :], in_send.at[t, lane, 2], q_sem.at[0], to
            ).wait_send()

    each_target(send_kv, 0, AHEAD)

    def prefix_copies(p, mine):
        whose = core if mine else other
        rows = pl.ds(pl.multiple_of((2 * xp + whose) * COLUMN + p * CHIP, CHIP), CHIP)
        cols = pl.ds(pl.multiple_of(flip * HEAD_DIM, HEAD_DIM), HEAD_DIM)
        for n, src in enumerate((pk_ref, pv_ref)):
            dst = window.at[0, pl.ds(p * CHIP, CHIP), pl.ds(n * HEAD_DIM, HEAD_DIM)]
            if mine:
                yield pltpu.make_async_copy(src.at[rows, cols], dst, kv_sem.at[0, p])
            else:
                yield remote(
                    src.at[rows, cols], dst, prefix_send.at[p, n], kv_sem.at[0, p],
                    device(y, x, z, other),
                )

    has_prefix = (y == 0) & (core == z_hi)

    @pl.when(has_prefix)
    def _():
        for p in range(CHIPS):
            for mine in (True, False):
                for copy in prefix_copies(p, mine):
                    copy.start()

    toward = jnp.where(z % 2 == 0, 1, 3)

    def piece_at(i):
        return (z // 2 + jnp.where(i == 0, 2, jnp.where(i == 1, toward, jnp.where(i == 2, -toward, 0))) + 4) % 4

    def routes(slot):
        across = device(y, x, z, other)
        near = device(y, x_near, z, core)
        if slot == 4:
            return (
                (y < 3, device((y + 1) % 4, x, z, core), 0, 0),
                (xp == 0, near, 2, 1),
                (core == 0, across, 3, 2),
            )
        if slot == 0:
            return ((xp == 1, near, 2, 1), (core == 1, across, 1, 3))
        return ((core == 0, across, 1, 3), (core == 1, across, 3, 2))

    def arrived(slot, p):
        rows = pl.ds(pl.multiple_of(p * CHIP, CHIP), CHIP)
        ref = window.at[slot, rows, :]
        pltpu.make_async_copy(ref, ref, kv_sem.at[slot, p]).wait()

    def forward(slot, p, start):
        rows = pl.ds(pl.multiple_of(p * CHIP, CHIP), CHIP)
        for condition, to, there, n in routes(slot):

            @pl.when(condition)
            def _():
                copy = remote(
                    window.at[slot, rows, :], window.at[there, rows, :],
                    fwd_send.at[n, p], kv_sem.at[there, p], to,
                )
                copy.start() if start else copy.wait_send()

    def build(slot, p):
        rows = pl.ds(pl.multiple_of(p * CHIP, CHIP), CHIP)
        at = pl.ds(pl.multiple_of(slot * COLUMN + p * CHIP, CHIP), CHIP)
        k = window[slot, rows, 0:HEAD_DIM]
        keys2[at, 0:HEAD_DIM] = k
        keys2[at, HEAD_DIM:PAIR] = k
        values2[at, 0:HEAD_DIM] = window[slot, rows, HEAD_DIM:PAIR]

    def relay(i, carry):
        for lag, slot in ((0, 4), (2, 0), (4, 2)):

            @pl.when((i >= lag) & (i < lag + CHIPS))
            def _():
                p = (z - ring_offset(i - lag) + 8) % 8
                arrived(slot, p)
                forward(slot, p, True)
                build(slot, p)
            if slot == 4:
                pl.when(i + AHEAD < 8)(lambda: targets(send_kv, i + AHEAD))
                early = i + AHEAD - 8
                for n in range(2):
                    pl.when((early >= 0) & (early < 4))(lambda: targets(send_q, 2 * early + n))

        return carry

    lax.fori_loop(0, CHIPS + 5, relay, 0)

    def last(i, carry):
        for slot in (3, 1):
            p = (z - ring_offset(i) + 8) % 8
            arrived(slot, p)
            build(slot, p)
        return carry

    lax.fori_loop(0, CHIPS, last, 0)

    @pl.when(y == 0)
    def _():
        first_row = WINDOW - my_column * COLUMN - start_ref[0]
        spare = window[4, 0:1, 0:HEAD_DIM].astype(jnp.float32)

        def fix(i, carry):
            at = pl.ds(pl.multiple_of(i * PIECE, PIECE), PIECE)
            real = i * PIECE + lax.broadcasted_iota(jnp.int32, (PIECE, HEAD_DIM), 0) >= first_row
            k = jnp.where(real, keys2[at, 0:HEAD_DIM].astype(jnp.float32), spare).astype(jnp.bfloat16)
            v = jnp.where(real, values2[at, 0:HEAD_DIM].astype(jnp.float32), 0.0)
            keys2[at, 0:HEAD_DIM] = k
            keys2[at, HEAD_DIM:PAIR] = k
            values2[at, 0:HEAD_DIM] = v.astype(jnp.bfloat16)
            values2[at, HEAD_DIM:PAIR] = jnp.where(real, 1.0, 0.0).astype(jnp.bfloat16)
            return carry

        lax.fori_loop(0, WINDOW // PIECE, fix, 0)

    scores = (even_scores, odd_scores)
    peaks = (even_peaks, odd_peaks)

    def queries(i):
        p = piece_at(i)
        rows = pl.ds(pl.multiple_of(p * PIECE, PIECE), PIECE)
        ref = q_in.at[rows, :]
        pltpu.make_async_copy(ref, ref, q_sem.at[p]).wait()
        for h in range(2):
            scaled = q_in[rows, h * HEAD_DIM : (h + 1) * HEAD_DIM].astype(jnp.float32) * LOG2E_SCALED
            high = scaled.astype(jnp.bfloat16)
            q2[h * PIECE : (h + 1) * PIECE, 0:HEAD_DIM] = high
            q2[h * PIECE : (h + 1) * PIECE, HEAD_DIM:PAIR] = (
                scaled - high.astype(jnp.float32)
            ).astype(jnp.bfloat16)

    def score(i, slot, step, peak):
        p = piece_at(i)
        at = pl.ds(pl.multiple_of((p + step) * PIECE, PIECE), PIECE)
        s = lax.dot_general(q2[...], keys2[at, :], NT, preferred_element_type=jnp.float32)
        if step in (0, STEPS - 1):
            token = lax.broadcasted_iota(jnp.int32, s.shape, 0) % PIECE
            key = lax.broadcasted_iota(jnp.int32, s.shape, 1)
            s = jnp.where(key > token if step == 0 else key <= token, s, MASKED)
        scores[slot][:, step * PIECE : (step + 1) * PIECE] = s
        for lane in range(0, PIECE, HEAD_DIM):
            peak = jnp.maximum(peak, s[:, lane : lane + HEAD_DIM])
        return peak

    def no_peak():
        return jnp.full((2 * PIECE, HEAD_DIM), MASKED, jnp.float32)

    def keep_peak(slot, peak):
        peaks[slot][...] = jnp.broadcast_to(jnp.max(peak, axis=1, keepdims=True), peak.shape)

    def mix(i, slot, step):
        p = piece_at(i)
        at = pl.ds(pl.multiple_of((p + step) * PIECE, PIECE), PIECE)
        peak = peaks[slot][...]
        weights = [
            jnp.exp2(scores[slot][:, lane : lane + HEAD_DIM] - peak).astype(jnp.bfloat16)
            for lane in range(step * PIECE, (step + 1) * PIECE, HEAD_DIM)
        ]
        return jnp.dot(
            jnp.concatenate(weights, axis=1), values2[at, :], preferred_element_type=jnp.float32
        )

    def home_copies(i, start):
        p = piece_at(i)
        cols = pl.ds(pl.multiple_of(my_head * PAIR, PAIR), PAIR)
        for n in range(4):
            z_, core_ = 2 * p + n // 2, n % 2
            mine = (my_column == x) & (z_ == z) & (core_ == core)
            src = o_out.at[p, pl.ds(n * ROWS, ROWS), :]
            dst = out_ref.at[:, cols]

            @pl.when(mine)
            def _():
                if start:
                    pltpu.make_async_copy(src, dst, o_sem).start()

            @pl.when(jnp.logical_not(mine))
            def _():
                copy = remote(src, dst, o_send.at[p, n], o_sem, device(y, my_column, z_, core_))
                copy.start() if start else copy.wait_send()

    def finish(i, total):
        p = piece_at(i)
        o = total[:, 0:HEAD_DIM] / total[:, HEAD_DIM:PAIR]
        o_out[p, :, 0:HEAD_DIM] = o[0:PIECE].astype(jnp.bfloat16)
        o_out[p, :, HEAD_DIM:PAIR] = o[PIECE:].astype(jnp.bfloat16)
        home_copies(i, True)

    queries(0)
    peak = no_peak()
    for step in range(STEPS):
        peak = score(0, 0, step, peak)
    keep_peak(0, peak)

    for i in range(PIECES - 1):
        slot = i % 2
        queries(i + 1)
        peak = no_peak()
        total = None
        for step in range(STEPS):
            peak = score(i + 1, 1 - slot, step, peak)
            part = mix(i, slot, step)
            total = part if total is None else total + part
        keep_peak(1 - slot, peak)
        finish(i, total)

    total = None
    for step in range(STEPS):
        part = mix(PIECES - 1, (PIECES - 1) % 2, step)
        total = part if total is None else total + part
    finish(PIECES - 1, total)

    pltpu.make_async_copy(out_ref, out_ref, o_sem).wait()
    each_target(sent)

    @pl.when(has_prefix)
    def _():
        for p in range(CHIPS):
            for copy in prefix_copies(p, False):
                copy.wait_send()

    def forwarded(p, carry):
        for slot in (4, 0, 2):
            forward(slot, p, False)
        return carry

    lax.fori_loop(0, CHIPS, forwarded, 0)
    for i in range(PIECES):
        home_copies(i, False)


def shards(queries, keys, values, prefix_keys, prefix_values, span_start):
    anywhere = pl.BlockSpec(memory_space=pl.ANY)
    return pl.pallas_call(
        kernel,
        out_shape=pltpu.VMEM(queries.shape, jnp.bfloat16),
        in_specs=[pl.BlockSpec(memory_space=pltpu.SMEM)] + [anywhere] * 5,
        out_specs=pl.BlockSpec(memory_space=pltpu.VMEM),
        scratch_shapes=[
            pltpu.VMEM((SLOTS, COLUMN, PAIR), jnp.bfloat16),
            pltpu.VMEM((COLUMN, PAIR), jnp.bfloat16),
            pltpu.VMEM((SLOTS * COLUMN, PAIR), jnp.bfloat16),
            pltpu.VMEM((SLOTS * COLUMN, PAIR), jnp.bfloat16),
            pltpu.VMEM((2 * PIECE, PAIR), jnp.bfloat16),
            pltpu.VMEM((2 * PIECE, SPAN), jnp.float32),
            pltpu.VMEM((2 * PIECE, SPAN), jnp.float32),
            pltpu.VMEM((2 * PIECE, HEAD_DIM), jnp.float32),
            pltpu.VMEM((2 * PIECE, HEAD_DIM), jnp.float32),
            pltpu.VMEM((PIECES, PIECE, PAIR), jnp.bfloat16),
            pltpu.SemaphoreType.DMA((SLOTS, CHIPS)),
            pltpu.SemaphoreType.DMA((PIECES,)),
            pltpu.SemaphoreType.DMA,
            pltpu.SemaphoreType.DMA((8, 2, 3)),
            pltpu.SemaphoreType.DMA((4, CHIPS)),
            pltpu.SemaphoreType.DMA((CHIPS, 2)),
            pltpu.SemaphoreType.DMA((PIECES, 4)),
        ],
        compiler_params=pltpu.CompilerParams(
            collective_id=0, has_side_effects=True, vmem_limit_bytes=60 << 20
        ),
    )(span_start, queries, keys, values, prefix_keys, prefix_values)


def solution(mesh):
    placed = (
        P(("seq", "head"), None),
        P(("seq", "head"), None),
        P(("seq", "head"), None),
        P(None, "head"),
        P(None, "head"),
        P(),
    )
    return jax.shard_map(
        shards, mesh=mesh, in_specs=placed, out_specs=P(("seq", "head"), None), check_vma=False
    )
```

```python
import functools
import math

import jax
import jax.numpy as jnp
from jax import lax
from jax.experimental import pallas as pl
from jax.experimental.pallas import tpu as pltpu
from jax.sharding import PartitionSpec as P

HEAD_DIM = 128
QH = 32
KVH = 16
QSCALE = 144
WINDOW = 4096

LOGICAL = pl.DeviceIdType.LOGICAL
ROWS = 64
COLUMN = 1024
PIECE = 256
PIECES = COLUMN // PIECE
CHIP = 128
CHIPS = COLUMN // CHIP
AHEAD = 6
SLOTS = 5
SPAN = WINDOW + PIECE
STEPS = SPAN // PIECE
PAIR = 2 * HEAD_DIM
MASKED = -1e30
LOG2E_SCALED = math.log2(math.e) * QSCALE ** (-0.5)
NT = (((1,), (1,)), ((), ()))


def ring_offset(t):
    half = (t + 1) // 2
    return jnp.where(t % 2 == 1, half, -half)


def kernel(
    start_ref, q_ref, k_ref, v_ref, pk_ref, pv_ref, out_ref,
    window, q_in, keys2, values2, q2, even_scores, odd_scores, even_peaks, odd_peaks, o_out,
    kv_sem, q_sem, o_sem, in_send, fwd_send, prefix_send, o_send,
):
    seq, head = lax.axis_index("seq"), lax.axis_index("head")
    y, x, z = seq // 8, (seq // 2) % 4, (seq % 2) * 4 + head // 2
    core = head % 2
    z_hi = seq % 2
    xp, xl = x // 2, x % 2
    other = 1 - core
    my_column = 2 * xp + core
    flip = (xl + xp) % 2

    def device(y_, x_, z_, core_):
        return y_ * 64 + x_ * 16 + z_ * 2 + core_

    def chip_head(x_, z_):
        return (z_ % 4) * 4 + (z_ // 4) * 2 + (x_ % 2 + x_ // 2) % 2

    my_head = chip_head(x, z)
    x_near = 3 - x

    def remote(src, dst, send, recv, to):
        return pltpu.make_async_remote_copy(
            src_ref=src, dst_ref=dst, send_sem=send, recv_sem=recv,
            device_id=to, device_id_type=LOGICAL,
        )

    barrier = pltpu.get_barrier_semaphore()

    def greet(to):
        pl.semaphore_signal(barrier, inc=1, device_id=to, device_id_type=LOGICAL)

    group = device(y, 2 * xp, 0, 0)
    place = device(0, xl, z, core)
    for i in range(16, 48):
        if i != 32:
            greet(group + lax.rem(place + i, 32))
    greet(device(y, x_near, z, core))
    greet(device((y + 1) % 4, x, z, core))
    greet(device((y + 3) % 4, x, z, core))
    values2[:, HEAD_DIM:PAIR] = jnp.ones((SLOTS * COLUMN, HEAD_DIM), jnp.bfloat16)
    pl.semaphore_wait(barrier, 34)

    my_rows = pl.ds(pl.multiple_of((z * 2 + core) * ROWS, ROWS), ROWS)

    def targets(body, t):
        z_ = (z + ring_offset(t) + 8) % 8
        for lane in range(2):
            x_ = 2 * xp + lane
            mine = (t == 0) & (xl == lane) & (core == xl)
            body(t, lane, x_, z_, mine)

    def each_target(body, first=0, stop=8):
        def at(t, carry):
            targets(body, t)
            return carry

        lax.fori_loop(first, stop, at, 0)

    def send_kv(t, lane, x_, z_, mine):
        h = chip_head(x_, z_)
        cols = pl.ds(pl.multiple_of(h * HEAD_DIM, HEAD_DIM), HEAD_DIM)
        for n, src in enumerate((k_ref, v_ref)):
            dst = window.at[4, my_rows, pl.ds(n * HEAD_DIM, HEAD_DIM)]
            recv = kv_sem.at[4, z]

            @pl.when(mine)
            def _():
                pltpu.make_async_copy(src.at[:, cols], dst, recv).start()

            @pl.when(jnp.logical_not(mine))
            def _():
                remote(
                    src.at[:, cols], dst, in_send.at[t, lane, n], recv, device(y, x_, z_, xl)
                ).start()

    def send_q(t, lane, x_, z_, mine):
        h = chip_head(x_, z_)
        cols = pl.ds(pl.multiple_of(h * PAIR, PAIR), PAIR)
        dst = q_in.at[my_rows, :]
        recv = q_sem.at[z // 2]

        @pl.when(mine)
        def _():
            pltpu.make_async_copy(q_ref.at[:, cols], dst, recv).start()

        @pl.when(jnp.logical_not(mine))
        def _():
            remote(
                q_ref.at[:, cols], dst, in_send.at[t, lane, 2], recv, device(y, x_, z_, xl)
            ).start()

    def sent(t, lane, x_, z_, mine):
        @pl.when(jnp.logical_not(mine))
        def _():
            to = device(y, x_, z_, xl)
            for n, src in enumerate((k_ref, v_ref)):
                cols = pl.ds(0, HEAD_DIM)
                dst = window.at[4, my_rows, pl.ds(n * HEAD_DIM, HEAD_DIM)]
                remote(src.at[:, cols], dst, in_send.at[t, lane, n], kv_sem.at[4, 0], to).wait_send()
            remote(
                q_ref.at[:, pl.ds(0, PAIR)], q_in.at[my_rows, :], in_send.at[t, lane, 2], q_sem.at[0], to
            ).wait_send()

    each_target(send_kv, 0, AHEAD)

    def prefix_copies(p, mine):
        whose = core if mine else other
        rows = pl.ds(pl.multiple_of((2 * xp + whose) * COLUMN + p * CHIP, CHIP), CHIP)
        cols = pl.ds(pl.multiple_of(flip * HEAD_DIM, HEAD_DIM), HEAD_DIM)
        for n, src in enumerate((pk_ref, pv_ref)):
            dst = window.at[0, pl.ds(p * CHIP, CHIP), pl.ds(n * HEAD_DIM, HEAD_DIM)]
            if mine:
                yield pltpu.make_async_copy(src.at[rows, cols], dst, kv_sem.at[0, p])
            else:
                yield remote(
                    src.at[rows, cols], dst, prefix_send.at[p, n], kv_sem.at[0, p],
                    device(y, x, z, other),
                )

    has_prefix = (y == 0) & (core == z_hi)

    @pl.when(has_prefix)
    def _():
        for p in range(CHIPS):
            for mine in (True, False):
                for copy in prefix_copies(p, mine):
                    copy.start()

    toward = jnp.where(z % 2 == 0, 1, 3)

    def piece_at(i):
        return (z // 2 + jnp.where(i == 0, 2, jnp.where(i == 1, toward, jnp.where(i == 2, -toward, 0))) + 4) % 4

    def routes(slot):
        across = device(y, x, z, other)
        near = device(y, x_near, z, core)
        if slot == 4:
            return (
                (y < 3, device((y + 1) % 4, x, z, core), 0, 0),
                (xp == 0, near, 2, 1),
                (core == 0, across, 3, 2),
            )
        if slot == 0:
            return ((xp == 1, near, 2, 1), (core == 1, across, 1, 3))
        return ((core == 0, across, 1, 3), (core == 1, across, 3, 2))

    def arrived(slot, p):
        rows = pl.ds(pl.multiple_of(p * CHIP, CHIP), CHIP)
        ref = window.at[slot, rows, :]
        pltpu.make_async_copy(ref, ref, kv_sem.at[slot, p]).wait()

    def forward(slot, p, start):
        rows = pl.ds(pl.multiple_of(p * CHIP, CHIP), CHIP)
        for condition, to, there, n in routes(slot):

            @pl.when(condition)
            def _():
                copy = remote(
                    window.at[slot, rows, :], window.at[there, rows, :],
                    fwd_send.at[n, p], kv_sem.at[there, p], to,
                )
                copy.start() if start else copy.wait_send()

    def build(slot, p):
        rows = pl.ds(pl.multiple_of(p * CHIP, CHIP), CHIP)
        at = pl.ds(pl.multiple_of(slot * COLUMN + p * CHIP, CHIP), CHIP)
        k = window[slot, rows, 0:HEAD_DIM]
        keys2[at, 0:HEAD_DIM] = k
        keys2[at, HEAD_DIM:PAIR] = k
        values2[at, 0:HEAD_DIM] = window[slot, rows, HEAD_DIM:PAIR]

    def relay(i, carry):
        for lag, slot in ((0, 4), (2, 0), (4, 2)):

            @pl.when((i >= lag) & (i < lag + CHIPS))
            def _():
                p = (z - ring_offset(i - lag) + 8) % 8
                arrived(slot, p)
                forward(slot, p, True)
                build(slot, p)
            if slot == 4:
                pl.when(i + AHEAD < 8)(lambda: targets(send_kv, i + AHEAD))
                early = i + AHEAD - 8
                for n in range(2):
                    pl.when((early >= 0) & (early < 4))(lambda: targets(send_q, 2 * early + n))

        return carry

    lax.fori_loop(0, CHIPS + 5, relay, 0)

    def last(i, carry):
        for slot in (3, 1):
            p = (z - ring_offset(i) + 8) % 8
            arrived(slot, p)
            build(slot, p)
        return carry

    lax.fori_loop(0, CHIPS, last, 0)

    @pl.when(y == 0)
    def _():
        first_row = WINDOW - my_column * COLUMN - start_ref[0]
        spare = window[4, 0:1, 0:HEAD_DIM].astype(jnp.float32)

        def fix(i, carry):
            at = pl.ds(pl.multiple_of(i * PIECE, PIECE), PIECE)
            real = i * PIECE + lax.broadcasted_iota(jnp.int32, (PIECE, HEAD_DIM), 0) >= first_row
            k = jnp.where(real, keys2[at, 0:HEAD_DIM].astype(jnp.float32), spare).astype(jnp.bfloat16)
            v = jnp.where(real, values2[at, 0:HEAD_DIM].astype(jnp.float32), 0.0)
            keys2[at, 0:HEAD_DIM] = k
            keys2[at, HEAD_DIM:PAIR] = k
            values2[at, 0:HEAD_DIM] = v.astype(jnp.bfloat16)
            values2[at, HEAD_DIM:PAIR] = jnp.where(real, 1.0, 0.0).astype(jnp.bfloat16)
            return carry

        lax.fori_loop(0, WINDOW // PIECE, fix, 0)

    scores = (even_scores, odd_scores)
    peaks = (even_peaks, odd_peaks)

    def queries(i):
        p = piece_at(i)
        rows = pl.ds(pl.multiple_of(p * PIECE, PIECE), PIECE)
        ref = q_in.at[rows, :]
        pltpu.make_async_copy(ref, ref, q_sem.at[p]).wait()
        for h in range(2):
            scaled = q_in[rows, h * HEAD_DIM : (h + 1) * HEAD_DIM].astype(jnp.float32) * LOG2E_SCALED
            high = scaled.astype(jnp.bfloat16)
            q2[h * PIECE : (h + 1) * PIECE, 0:HEAD_DIM] = high
            q2[h * PIECE : (h + 1) * PIECE, HEAD_DIM:PAIR] = (
                scaled - high.astype(jnp.float32)
            ).astype(jnp.bfloat16)

    def score(i, slot, step, peak):
        p = piece_at(i)
        at = pl.ds(pl.multiple_of((p + step) * PIECE, PIECE), PIECE)
        s = lax.dot_general(q2[...], keys2[at, :], NT, preferred_element_type=jnp.float32)
        if step in (0, STEPS - 1):
            token = lax.broadcasted_iota(jnp.int32, s.shape, 0) % PIECE
            key = lax.broadcasted_iota(jnp.int32, s.shape, 1)
            s = jnp.where(key > token if step == 0 else key <= token, s, MASKED)
        scores[slot][:, step * PIECE : (step + 1) * PIECE] = s
        for lane in range(0, PIECE, HEAD_DIM):
            peak = jnp.maximum(peak, s[:, lane : lane + HEAD_DIM])
        return peak

    def no_peak():
        return jnp.full((2 * PIECE, HEAD_DIM), MASKED, jnp.float32)

    def keep_peak(slot, peak):
        peaks[slot][...] = jnp.broadcast_to(jnp.max(peak, axis=1, keepdims=True), peak.shape)

    def mix(i, slot, step):
        p = piece_at(i)
        at = pl.ds(pl.multiple_of((p + step) * PIECE, PIECE), PIECE)
        peak = peaks[slot][...]
        weights = [
            jnp.exp2(scores[slot][:, lane : lane + HEAD_DIM] - peak).astype(jnp.bfloat16)
            for lane in range(step * PIECE, (step + 1) * PIECE, HEAD_DIM)
        ]
        return jnp.dot(
            jnp.concatenate(weights, axis=1), values2[at, :], preferred_element_type=jnp.float32
        )

    def home_copies(i, start):
        p = piece_at(i)
        cols = pl.ds(pl.multiple_of(my_head * PAIR, PAIR), PAIR)
        for n in range(4):
            z_, core_ = 2 * p + n // 2, n % 2
            mine = (my_column == x) & (z_ == z) & (core_ == core)
            src = o_out.at[p, pl.ds(n * ROWS, ROWS), :]
            dst = out_ref.at[:, cols]

            @pl.when(mine)
            def _():
                if start:
                    pltpu.make_async_copy(src, dst, o_sem).start()

            @pl.when(jnp.logical_not(mine))
            def _():
                copy = remote(src, dst, o_send.at[p, n], o_sem, device(y, my_column, z_, core_))
                copy.start() if start else copy.wait_send()

    def finish(i, total):
        p = piece_at(i)
        o = total[:, 0:HEAD_DIM] / total[:, HEAD_DIM:PAIR]
        o_out[p, :, 0:HEAD_DIM] = o[0:PIECE].astype(jnp.bfloat16)
        o_out[p, :, HEAD_DIM:PAIR] = o[PIECE:].astype(jnp.bfloat16)
        home_copies(i, True)

    queries(0)
    peak = no_peak()
    for step in range(STEPS):
        peak = score(0, 0, step, peak)
    keep_peak(0, peak)

    for i in range(PIECES - 1):
        slot = i % 2
        queries(i + 1)
        peak = no_peak()
        total = None
        for step in range(STEPS):
            peak = score(i + 1, 1 - slot, step, peak)
            part = mix(i, slot, step)
            total = part if total is None else total + part
        keep_peak(1 - slot, peak)
        finish(i, total)

    total = None
    for step in range(STEPS):
        part = mix(PIECES - 1, (PIECES - 1) % 2, step)
        total = part if total is None else total + part
    finish(PIECES - 1, total)

    each_target(sent)

    @pl.when(has_prefix)
    def _():
        for p in range(CHIPS):
            for copy in prefix_copies(p, False):
                copy.wait_send()

    def forwarded(p, carry):
        for slot in (4, 0, 2):
            forward(slot, p, False)
        return carry

    lax.fori_loop(0, CHIPS, forwarded, 0)
    for i in range(PIECES):
        home_copies(i, False)
    pltpu.make_async_copy(out_ref, out_ref, o_sem).wait()


def shards(queries, keys, values, prefix_keys, prefix_values, span_start):
    anywhere = pl.BlockSpec(memory_space=pl.ANY)
    return pl.pallas_call(
        kernel,
        out_shape=pltpu.VMEM(queries.shape, jnp.bfloat16),
        in_specs=[pl.BlockSpec(memory_space=pltpu.SMEM)] + [anywhere] * 5,
        out_specs=pl.BlockSpec(memory_space=pltpu.VMEM),
        scratch_shapes=[
            pltpu.VMEM((SLOTS, COLUMN, PAIR), jnp.bfloat16),
            pltpu.VMEM((COLUMN, PAIR), jnp.bfloat16),
            pltpu.VMEM((SLOTS * COLUMN, PAIR), jnp.bfloat16),
            pltpu.VMEM((SLOTS * COLUMN, PAIR), jnp.bfloat16),
            pltpu.VMEM((2 * PIECE, PAIR), jnp.bfloat16),
            pltpu.VMEM((2 * PIECE, SPAN), jnp.float32),
            pltpu.VMEM((2 * PIECE, SPAN), jnp.float32),
            pltpu.VMEM((2 * PIECE, HEAD_DIM), jnp.float32),
            pltpu.VMEM((2 * PIECE, HEAD_DIM), jnp.float32),
            pltpu.VMEM((PIECES, PIECE, PAIR), jnp.bfloat16),
            pltpu.SemaphoreType.DMA((SLOTS, CHIPS)),
            pltpu.SemaphoreType.DMA((PIECES,)),
            pltpu.SemaphoreType.DMA,
            pltpu.SemaphoreType.DMA((8, 2, 3)),
            pltpu.SemaphoreType.DMA((4, CHIPS)),
            pltpu.SemaphoreType.DMA((CHIPS, 2)),
            pltpu.SemaphoreType.DMA((PIECES, 4)),
        ],
        compiler_params=pltpu.CompilerParams(
            collective_id=0, has_side_effects=True, vmem_limit_bytes=60 << 20
        ),
    )(span_start, queries, keys, values, prefix_keys, prefix_values)


def solution(mesh):
    placed = (
        P(("seq", "head"), None),
        P(("seq", "head"), None),
        P(("seq", "head"), None),
        P(None, "head"),
        P(None, "head"),
        P(),
    )
    return jax.shard_map(
        shards, mesh=mesh, in_specs=placed, out_specs=P(("seq", "head"), None), check_vma=False
    )
```

```python
import functools
import math

import jax
import jax.numpy as jnp
from jax import lax
from jax.experimental import pallas as pl
from jax.experimental.pallas import tpu as pltpu
from jax.sharding import PartitionSpec as P

HEAD_DIM = 128
QH = 32
KVH = 16
QSCALE = 144
WINDOW = 4096

LOGICAL = pl.DeviceIdType.LOGICAL
ROWS = 64
COLUMN = 1024
PIECE = 256
PIECES = COLUMN // PIECE
CHIP = 128
CHIPS = COLUMN // CHIP
AHEAD = 6
SLOTS = 5
SPAN = WINDOW + PIECE
STEPS = SPAN // PIECE
PAIR = 2 * HEAD_DIM
MASKED = -1e30
LOG2E_SCALED = math.log2(math.e) * QSCALE ** (-0.5)
NT = (((1,), (1,)), ((), ()))


def ring_offset(t):
    half = (t + 1) // 2
    return jnp.where(t % 2 == 1, half, -half)


def kernel(
    start_ref, q_ref, k_ref, v_ref, pk_ref, pv_ref, out_ref,
    window, q_in, keys2, values2, q2, even_scores, odd_scores, even_peaks, odd_peaks, o_out,
    kv_sem, q_sem, o_sem, in_send, fwd_send, prefix_send, o_send,
):
    seq, head = lax.axis_index("seq"), lax.axis_index("head")
    y, x, z = seq // 8, (seq // 2) % 4, (seq % 2) * 4 + head // 2
    core = head % 2
    z_hi = seq % 2
    xp, xl = x // 2, x % 2
    other = 1 - core
    my_column = 2 * xp + core
    flip = (xl + xp) % 2

    def device(y_, x_, z_, core_):
        return y_ * 64 + x_ * 16 + z_ * 2 + core_

    def chip_head(x_, z_):
        return (z_ % 4) * 4 + (z_ // 4) * 2 + (x_ % 2 + x_ // 2) % 2

    my_head = chip_head(x, z)
    x_near = 3 - x

    def remote(src, dst, send, recv, to):
        return pltpu.make_async_remote_copy(
            src_ref=src, dst_ref=dst, send_sem=send, recv_sem=recv,
            device_id=to, device_id_type=LOGICAL,
        )

    barrier = pltpu.get_barrier_semaphore()

    def greet(to):
        pl.semaphore_signal(barrier, inc=1, device_id=to, device_id_type=LOGICAL)

    group = device(y, 2 * xp, 0, 0)
    place = device(0, xl, z, core)
    for i in range(16, 48):
        if i != 32:
            greet(group + lax.rem(place + i, 32))
    greet(device(y, x_near, z, core))
    greet(device((y + 1) % 4, x, z, core))
    greet(device((y + 3) % 4, x, z, core))
    values2[:, HEAD_DIM:PAIR] = jnp.ones((SLOTS * COLUMN, HEAD_DIM), jnp.bfloat16)
    pl.semaphore_wait(barrier, 34)

    my_rows = pl.ds(pl.multiple_of((z * 2 + core) * ROWS, ROWS), ROWS)

    def targets(body, t):
        z_ = (z + ring_offset(t) + 8) % 8
        for lane in range(2):
            x_ = 2 * xp + lane
            mine = (t == 0) & (xl == lane) & (core == xl)
            body(t, lane, x_, z_, mine)

    def each_target(body, first=0, stop=8):
        def at(t, carry):
            targets(body, t)
            return carry

        lax.fori_loop(first, stop, at, 0)

    def send_kv(t, lane, x_, z_, mine):
        h = chip_head(x_, z_)
        cols = pl.ds(pl.multiple_of(h * HEAD_DIM, HEAD_DIM), HEAD_DIM)
        for n, src in enumerate((k_ref, v_ref)):
            dst = window.at[4, my_rows, pl.ds(n * HEAD_DIM, HEAD_DIM)]
            recv = kv_sem.at[4, z]

            @pl.when(mine)
            def _():
                pltpu.make_async_copy(src.at[:, cols], dst, recv).start()

            @pl.when(jnp.logical_not(mine))
            def _():
                remote(
                    src.at[:, cols], dst, in_send.at[t, lane, n], recv, device(y, x_, z_, xl)
                ).start()

    def send_q(t, lane, x_, z_, mine):
        h = chip_head(x_, z_)
        cols = pl.ds(pl.multiple_of(h * PAIR, PAIR), PAIR)
        dst = q_in.at[my_rows, :]
        recv = q_sem.at[z // 2]

        @pl.when(mine)
        def _():
            pltpu.make_async_copy(q_ref.at[:, cols], dst, recv).start()

        @pl.when(jnp.logical_not(mine))
        def _():
            remote(
                q_ref.at[:, cols], dst, in_send.at[t, lane, 2], recv, device(y, x_, z_, xl)
            ).start()

    def sent(t, lane, x_, z_, mine):
        @pl.when(jnp.logical_not(mine))
        def _():
            to = device(y, x_, z_, xl)
            for n, src in enumerate((k_ref, v_ref)):
                cols = pl.ds(0, HEAD_DIM)
                dst = window.at[4, my_rows, pl.ds(n * HEAD_DIM, HEAD_DIM)]
                remote(src.at[:, cols], dst, in_send.at[t, lane, n], kv_sem.at[4, 0], to).wait_send()
            remote(
                q_ref.at[:, pl.ds(0, PAIR)], q_in.at[my_rows, :], in_send.at[t, lane, 2], q_sem.at[0], to
            ).wait_send()

    each_target(send_kv, 0, AHEAD)

    def prefix_copies(p, mine):
        whose = core if mine else other
        rows = pl.ds(pl.multiple_of((2 * xp + whose) * COLUMN + p * CHIP, CHIP), CHIP)
        cols = pl.ds(pl.multiple_of(flip * HEAD_DIM, HEAD_DIM), HEAD_DIM)
        for n, src in enumerate((pk_ref, pv_ref)):
            dst = window.at[0, pl.ds(p * CHIP, CHIP), pl.ds(n * HEAD_DIM, HEAD_DIM)]
            if mine:
                yield pltpu.make_async_copy(src.at[rows, cols], dst, kv_sem.at[0, p])
            else:
                yield remote(
                    src.at[rows, cols], dst, prefix_send.at[p, n], kv_sem.at[0, p],
                    device(y, x, z, other),
                )

    has_prefix = (y == 0) & (core == z_hi)

    @pl.when(has_prefix)
    def _():
        for p in range(CHIPS):
            for mine in (True, False):
                for copy in prefix_copies(p, mine):
                    copy.start()

    toward = jnp.where(z % 2 == 0, 1, 3)

    def piece_at(i):
        return (z // 2 + jnp.where(i == 0, 2, jnp.where(i == 1, toward, jnp.where(i == 2, -toward, 0))) + 4) % 4

    def routes(slot):
        across = device(y, x, z, other)
        near = device(y, x_near, z, core)
        if slot == 4:
            return (
                (y < 3, device((y + 1) % 4, x, z, core), 0, 0),
                (xp == 0, near, 2, 1),
                (core == 0, across, 3, 2),
            )
        if slot == 0:
            return ((xp == 1, near, 2, 1), (core == 1, across, 1, 3))
        return ((core == 0, across, 1, 3), (core == 1, across, 3, 2))

    def arrived(slot, p):
        rows = pl.ds(pl.multiple_of(p * CHIP, CHIP), CHIP)
        ref = window.at[slot, rows, :]
        pltpu.make_async_copy(ref, ref, kv_sem.at[slot, p]).wait()

    def forward(slot, p, start):
        rows = pl.ds(pl.multiple_of(p * CHIP, CHIP), CHIP)
        for condition, to, there, n in routes(slot):

            @pl.when(condition)
            def _():
                copy = remote(
                    window.at[slot, rows, :], window.at[there, rows, :],
                    fwd_send.at[n, p], kv_sem.at[there, p], to,
                )
                copy.start() if start else copy.wait_send()

    def build(slot, p):
        rows = pl.ds(pl.multiple_of(p * CHIP, CHIP), CHIP)
        at = pl.ds(pl.multiple_of(slot * COLUMN + p * CHIP, CHIP), CHIP)
        k = window[slot, rows, 0:HEAD_DIM]
        keys2[at, 0:HEAD_DIM] = k
        keys2[at, HEAD_DIM:PAIR] = k
        values2[at, 0:HEAD_DIM] = window[slot, rows, HEAD_DIM:PAIR]

    def relay(i, carry):
        for lag, slot in ((0, 4), (2, 0), (4, 2)):

            @pl.when((i >= lag) & (i < lag + CHIPS))
            def _():
                p = (z - ring_offset(i - lag) + 8) % 8
                arrived(slot, p)
                forward(slot, p, True)
                build(slot, p)
            if slot == 4:
                pl.when(i + AHEAD < 8)(lambda: targets(send_kv, i + AHEAD))
                early = i + AHEAD - 8
                for n in range(2):
                    pl.when((early >= 0) & (early < 4))(lambda: targets(send_q, 2 * early + n))

        @pl.when(i >= 5)
        def _():
            p = (z - ring_offset(i - 5) + 8) % 8
            arrived(1 + 2 * core, p)
            build(1 + 2 * core, p)

        return carry

    lax.fori_loop(0, CHIPS + 5, relay, 0)

    def last(i, carry):
        p = (z - ring_offset(i) + 8) % 8
        arrived(3 - 2 * core, p)
        build(3 - 2 * core, p)
        return carry

    lax.fori_loop(0, CHIPS, last, 0)

    @pl.when(y == 0)
    def _():
        first_row = WINDOW - my_column * COLUMN - start_ref[0]
        spare = window[4, 0:1, 0:HEAD_DIM].astype(jnp.float32)

        def fix(i, carry):
            at = pl.ds(pl.multiple_of(i * PIECE, PIECE), PIECE)
            real = i * PIECE + lax.broadcasted_iota(jnp.int32, (PIECE, HEAD_DIM), 0) >= first_row
            k = jnp.where(real, keys2[at, 0:HEAD_DIM].astype(jnp.float32), spare).astype(jnp.bfloat16)
            v = jnp.where(real, values2[at, 0:HEAD_DIM].astype(jnp.float32), 0.0)
            keys2[at, 0:HEAD_DIM] = k
            keys2[at, HEAD_DIM:PAIR] = k
            values2[at, 0:HEAD_DIM] = v.astype(jnp.bfloat16)
            values2[at, HEAD_DIM:PAIR] = jnp.where(real, 1.0, 0.0).astype(jnp.bfloat16)
            return carry

        lax.fori_loop(0, WINDOW // PIECE, fix, 0)

    scores = (even_scores, odd_scores)
    peaks = (even_peaks, odd_peaks)

    def queries(i):
        p = piece_at(i)
        rows = pl.ds(pl.multiple_of(p * PIECE, PIECE), PIECE)
        ref = q_in.at[rows, :]
        pltpu.make_async_copy(ref, ref, q_sem.at[p]).wait()
        for h in range(2):
            scaled = q_in[rows, h * HEAD_DIM : (h + 1) * HEAD_DIM].astype(jnp.float32) * LOG2E_SCALED
            high = scaled.astype(jnp.bfloat16)
            q2[h * PIECE : (h + 1) * PIECE, 0:HEAD_DIM] = high
            q2[h * PIECE : (h + 1) * PIECE, HEAD_DIM:PAIR] = (
                scaled - high.astype(jnp.float32)
            ).astype(jnp.bfloat16)

    def score(i, slot, step, peak):
        p = piece_at(i)
        at = pl.ds(pl.multiple_of((p + step) * PIECE, PIECE), PIECE)
        s = lax.dot_general(q2[...], keys2[at, :], NT, preferred_element_type=jnp.float32)
        if step in (0, STEPS - 1):
            token = lax.broadcasted_iota(jnp.int32, s.shape, 0) % PIECE
            key = lax.broadcasted_iota(jnp.int32, s.shape, 1)
            s = jnp.where(key > token if step == 0 else key <= token, s, MASKED)
        scores[slot][:, step * PIECE : (step + 1) * PIECE] = s
        for lane in range(0, PIECE, HEAD_DIM):
            peak = jnp.maximum(peak, s[:, lane : lane + HEAD_DIM])
        return peak

    def no_peak():
        return jnp.full((2 * PIECE, HEAD_DIM), MASKED, jnp.float32)

    def keep_peak(slot, peak):
        peaks[slot][...] = jnp.broadcast_to(jnp.max(peak, axis=1, keepdims=True), peak.shape)

    def mix(i, slot, step):
        p = piece_at(i)
        at = pl.ds(pl.multiple_of((p + step) * PIECE, PIECE), PIECE)
        peak = peaks[slot][...]
        weights = [
            jnp.exp2(scores[slot][:, lane : lane + HEAD_DIM] - peak).astype(jnp.bfloat16)
            for lane in range(step * PIECE, (step + 1) * PIECE, HEAD_DIM)
        ]
        return jnp.dot(
            jnp.concatenate(weights, axis=1), values2[at, :], preferred_element_type=jnp.float32
        )

    def home_copies(i, start):
        p = piece_at(i)
        cols = pl.ds(pl.multiple_of(my_head * PAIR, PAIR), PAIR)
        for n in range(4):
            z_, core_ = 2 * p + n // 2, n % 2
            mine = (my_column == x) & (z_ == z) & (core_ == core)
            src = o_out.at[p, pl.ds(n * ROWS, ROWS), :]
            dst = out_ref.at[:, cols]

            @pl.when(mine)
            def _():
                if start:
                    pltpu.make_async_copy(src, dst, o_sem).start()

            @pl.when(jnp.logical_not(mine))
            def _():
                copy = remote(src, dst, o_send.at[p, n], o_sem, device(y, my_column, z_, core_))
                copy.start() if start else copy.wait_send()

    def finish(i, total):
        p = piece_at(i)
        o = total[:, 0:HEAD_DIM] / total[:, HEAD_DIM:PAIR]
        o_out[p, :, 0:HEAD_DIM] = o[0:PIECE].astype(jnp.bfloat16)
        o_out[p, :, HEAD_DIM:PAIR] = o[PIECE:].astype(jnp.bfloat16)
        home_copies(i, True)

    queries(0)
    peak = no_peak()
    for step in range(STEPS):
        peak = score(0, 0, step, peak)
    keep_peak(0, peak)

    for i in range(PIECES - 1):
        slot = i % 2
        queries(i + 1)
        peak = no_peak()
        total = None
        for step in range(STEPS):
            peak = score(i + 1, 1 - slot, step, peak)
            part = mix(i, slot, step)
            total = part if total is None else total + part
        keep_peak(1 - slot, peak)
        finish(i, total)

    total = None
    for step in range(STEPS):
        part = mix(PIECES - 1, (PIECES - 1) % 2, step)
        total = part if total is None else total + part
    finish(PIECES - 1, total)

    each_target(sent)

    @pl.when(has_prefix)
    def _():
        for p in range(CHIPS):
            for copy in prefix_copies(p, False):
                copy.wait_send()

    def forwarded(p, carry):
        for slot in (4, 0, 2):
            forward(slot, p, False)
        return carry

    lax.fori_loop(0, CHIPS, forwarded, 0)
    for i in range(PIECES):
        home_copies(i, False)
    pltpu.make_async_copy(out_ref, out_ref, o_sem).wait()


def shards(queries, keys, values, prefix_keys, prefix_values, span_start):
    anywhere = pl.BlockSpec(memory_space=pl.ANY)
    return pl.pallas_call(
        kernel,
        out_shape=pltpu.VMEM(queries.shape, jnp.bfloat16),
        in_specs=[pl.BlockSpec(memory_space=pltpu.SMEM)] + [anywhere] * 5,
        out_specs=pl.BlockSpec(memory_space=pltpu.VMEM),
        scratch_shapes=[
            pltpu.VMEM((SLOTS, COLUMN, PAIR), jnp.bfloat16),
            pltpu.VMEM((COLUMN, PAIR), jnp.bfloat16),
            pltpu.VMEM((SLOTS * COLUMN, PAIR), jnp.bfloat16),
            pltpu.VMEM((SLOTS * COLUMN, PAIR), jnp.bfloat16),
            pltpu.VMEM((2 * PIECE, PAIR), jnp.bfloat16),
            pltpu.VMEM((2 * PIECE, SPAN), jnp.float32),
            pltpu.VMEM((2 * PIECE, SPAN), jnp.float32),
            pltpu.VMEM((2 * PIECE, HEAD_DIM), jnp.float32),
            pltpu.VMEM((2 * PIECE, HEAD_DIM), jnp.float32),
            pltpu.VMEM((PIECES, PIECE, PAIR), jnp.bfloat16),
            pltpu.SemaphoreType.DMA((SLOTS, CHIPS)),
            pltpu.SemaphoreType.DMA((PIECES,)),
            pltpu.SemaphoreType.DMA,
            pltpu.SemaphoreType.DMA((8, 2, 3)),
            pltpu.SemaphoreType.DMA((4, CHIPS)),
            pltpu.SemaphoreType.DMA((CHIPS, 2)),
            pltpu.SemaphoreType.DMA((PIECES, 4)),
        ],
        compiler_params=pltpu.CompilerParams(
            collective_id=0, has_side_effects=True, vmem_limit_bytes=60 << 20
        ),
    )(span_start, queries, keys, values, prefix_keys, prefix_values)


def solution(mesh):
    placed = (
        P(("seq", "head"), None),
        P(("seq", "head"), None),
        P(("seq", "head"), None),
        P(None, "head"),
        P(None, "head"),
        P(),
    )
    return jax.shard_map(
        shards, mesh=mesh, in_specs=placed, out_specs=P(("seq", "head"), None), check_vma=False
    )
```
